128 devices in a mesh: pitch: 8 (over y, x_hi), span: 4 (over z), axial: 4 (over x_lo, core).
Axes of the slice: x: 4 (x_hi: 2, x_lo: 2; x = x_hi * 2 + x_lo), y: 4, z: 4, core: 2. Of those that a mesh axis runs over, the one named last changes fastest.
Arguments:
- guess: float32 [2, 6, 64, 64, 512], P(None, None, 'pitch', 'span', 'axial'), may hold values from -6 to 6
- right_side: float32 [2, 6, 64, 64, 512], P(None, None, 'pitch', 'span', 'axial'), may hold values from -60 to 60
- diag_block: bfloat16 [6, 6, 64, 64, 512], P(None, None, 'pitch', 'span', 'axial'), may hold values from -4 to 4
- neighbour_blocks: bfloat16 [6, 6, 6, 64, 64, 512], P(None, None, None, 'pitch', 'span', 'axial'), may hold values from -0.6484375 to 0.6484375
- dissipation: float32 [3, 64, 64, 512], P(None, 'pitch', 'span', 'axial'), may hold values from 0.03 to 0.25
- omega_volume: float32 [64, 64, 512], P('pitch', 'span', 'axial'), may hold values from 0.2 to 2
- pseudo_step: float32 [64, 64, 512], P('pitch', 'span', 'axial'), may hold values from 0.03 to 0.3
- phase: float32 [1], replicated, may hold values from -3.140625 to 3.140625
Outputs:
- solution_field: float32 [2, 6, 64, 64, 512], P(None, None, 'pitch', 'span', 'axial')
- norms: float32 [2], replicated
The draws below stay inside these ranges and needn't reach their ends.
All inputs are finite; a program needn't handle non-finite values.
Results may differ from the reference program's by a relative error of at most 0.0003.
Values sent between devices are 32-bit elements; how exact they have to be, the bound alone decides.
A program may use at most 128 MiB of HBM per device.

```python
import math
import jax
import jax.numpy as jnp

NV = 6
ITERS = 2
NP = 64
NS = 64
NA = 512


def wall_profile():
    rows = jnp.arange(NS, dtype=jnp.float32)
    distance = jnp.minimum(rows, float(NS - 1) - rows)
    return jnp.exp(-distance / 1.5)


def draw_right_side(key, part):
    key_base = jax.random.fold_in(key, 11)
    key_scale = jax.random.fold_in(key, 12)
    shape_all = (2, NV, NP, NS, NA)
    span_pos = jnp.arange(NS, dtype=jnp.float32) / max(NS - 1, 1)
    wall_factor = 1.0 + 2.5 * wall_profile()
    base = jnp.clip(jax.random.normal(key_base, shape_all, jnp.float32), -3.0, 3.0)
    ramp = 1.0 + 2.0 * span_pos
    scale = jnp.exp(jax.random.uniform(key_scale, shape_all, jnp.float32, 0.0, math.log(10.0))) / 6.0
    profile = ramp * wall_factor
    return (base * scale * profile[None, None, None, :, None]).astype(jnp.float32)


def draw_diag_block(key, part):
    key_off = jax.random.fold_in(key, 21)
    key_mag = jax.random.fold_in(key, 22)
    off_part = jnp.clip(0.35 * jax.random.normal(key_off, (NV, NV, NP, NS, NA), jnp.float32), -0.45, 0.45)
    magnitude = jax.random.uniform(key_mag, (NV, NP, NS, NA), jnp.float32, 2.5, 4.0)
    identity = jnp.eye(NV, dtype=jnp.float32)[:, :, None, None, None]
    return (off_part * (1.0 - identity) + identity * magnitude[:, None]).astype(jnp.bfloat16)


def draw_pseudo_step(key, part):
    key_step = jax.random.fold_in(key, 31)
    base = jnp.exp(jax.random.uniform(key_step, (NP, NS, NA), jnp.float32, math.log(0.1), math.log(0.3)))
    shrink = 1.0 + 2.0 * wall_profile()
    return (base / shrink[None, :, None]).astype(jnp.float32)


def block_levels(key, dims, split, smallest, largest):
    loudness, own = 1.0, jax.random.fold_in(key, 6)
    for axis_at, shards_of in split:
        heights = jnp.exp(jax.random.uniform(jax.random.fold_in(own, axis_at), (shards_of,), jnp.float32, smallest / len(split), largest / len(split)))
        loudness = loudness * jnp.repeat(heights, dims[axis_at] // shards_of).reshape([-1 if axis == axis_at else 1 for axis in range(len(dims))])
    return loudness


def scatter_about(rng, extent, spread, limit, shards=(), kind=jnp.bfloat16):
    values = jax.random.normal(rng, extent, jnp.float32) * spread
    if len(shards) > 0:
        values = block_levels(rng, extent, shards, -0.22, 0.18) * values
    return jnp.clip(values, min=-limit, max=limit).astype(kind)


def setup_inputs(seed: int = 0) -> dict:
    key_of = jax.random.split(jax.random.key(seed), 9)
    return {
        "guess": scatter_about(key_of[0], (2, NV, NP, NS, NA), 1.0, 6.0, ((2, 8), (3, 4), (4, 4)), jnp.float32),
        "right_side": draw_right_side(jax.random.fold_in(key_of[8], 71), 0),
        "diag_block": draw_diag_block(jax.random.fold_in(key_of[8], 71), 0),
        "neighbour_blocks": scatter_about(key_of[3], (6, NV, NV, NP, NS, NA), 0.26, 0.6484375, ((3, 8), (4, 4), (5, 4))),
        "dissipation": jnp.clip(jnp.exp(math.log(0.25) - 2.1202636 * jax.random.uniform(key_of[4], (3, NP, NS, NA), jnp.float32) ** block_levels(key_of[4], (3, NP, NS, NA), ((1, 8), (2, 4), (3, 4)), -0.2, 0.2)), 0.03, 0.25),
        "omega_volume": jnp.clip(jnp.exp(math.log(2.0) - 2.3025851 * jax.random.uniform(key_of[5], (NP, NS, NA), jnp.float32) ** block_levels(key_of[5], (NP, NS, NA), ((0, 8), (1, 4), (2, 4)), -0.2, 0.2)), 0.2, 2.0),
        "pseudo_step": draw_pseudo_step(jax.random.fold_in(key_of[8], 71), 0),
        "phase": jnp.clip(jax.random.uniform(key_of[7], (1,), jnp.float32, -3.140625, 3.140625), -3.140625, 3.140625),
    }


def block_apply(blocks, vector_in):
    summed = None
    for column in range(blocks.shape[1]):
        product = blocks[:, column].astype(jnp.float32)[None] * vector_in[:, column][:, None]
        summed = product if summed is None else summed + product
    return summed

def rotate(values, cosine, sine_part):
    real_part = values[0]
    imag_part = values[1]
    return jnp.stack([cosine * real_part - sine_part * imag_part, sine_part * real_part + cosine * imag_part])

def operate(current, pitch_ext, span_ext, axial_ext, diag_block, neighbour_blocks, dissipation, omega_volume):
    summed = block_apply(diag_block, current)
    summed = summed + block_apply(neighbour_blocks[0], pitch_ext[:, :, 1:-3]) + block_apply(neighbour_blocks[1], pitch_ext[:, :, 3:-1])
    summed = summed + block_apply(neighbour_blocks[2], span_ext[:, :, :, 1:-3]) + block_apply(neighbour_blocks[3], span_ext[:, :, :, 3:-1])
    summed = summed + block_apply(neighbour_blocks[4], axial_ext[:, :, :, :, 1:-3]) + block_apply(neighbour_blocks[5], axial_ext[:, :, :, :, 3:-1])
    summed = summed + dissipation[0] * (pitch_ext[:, :, :-4] + pitch_ext[:, :, 4:])
    summed = summed + dissipation[1] * (span_ext[:, :, :, :-4] + span_ext[:, :, :, 4:])
    summed = summed + dissipation[2] * (axial_ext[:, :, :, :, :-4] + axial_ext[:, :, :, :, 4:])
    rotation_term = jnp.stack([-omega_volume * current[1], omega_volume * current[0]])
    return summed + rotation_term

def reference(guess, right_side, diag_block, neighbour_blocks, dissipation, omega_volume, pseudo_step, phase):
    cosine = jnp.cos(phase[0])
    sine_part = jnp.sin(phase[0])
    current = guess
    square_sums = []
    for iteration in range(ITERS):
        pitch_ext = jnp.concatenate([rotate(current[:, :, -2:], cosine, -sine_part), current, rotate(current[:, :, :2], cosine, sine_part)], axis=2)
        span_ext = jnp.pad(current, ((0, 0), (0, 0), (0, 0), (2, 2), (0, 0)))
        axial_ext = jnp.pad(current, ((0, 0), (0, 0), (0, 0), (0, 0), (2, 2)))
        residual = right_side - operate(current, pitch_ext, span_ext, axial_ext, diag_block, neighbour_blocks, dissipation, omega_volume)
        square_sums.append(jnp.sum(residual * residual))
        current = current + pseudo_step[None, None] * residual
    cell_count = float(guess.size)
    norms = jnp.sqrt(jnp.stack(square_sums) / cell_count)
    return (current, norms)
```

```python
import functools

import jax
import jax.numpy as jnp
from jax import lax
from jax.experimental import pallas as pl
from jax.experimental.pallas import tpu as pltpu
from jax.sharding import PartitionSpec as P

ITERS = 2
MESH = pl.DeviceIdType.MESH
F32 = jnp.float32


def kernel(
    guess, right_h, diag_h, neigh_h, diss_h, omega_h, pseudo_h, phase,
    out, norms,
    st, hal, prt, rs, dg, nb, ds, om, ps, axs, axr, sq, red, tot_s,
    ld_sem, psend, precv, zsend, zrecv, asend, arecv, rsend, rrecv, ready,
):
    p, s, a = lax.axis_index("pitch"), lax.axis_index("span"), lax.axis_index("axial")
    size_p, size_s, size_a = lax.axis_size("pitch"), lax.axis_size("span"), lax.axis_size("axial")
    y, x_hi = p // 2, lax.rem(p, 2)
    lower, upper = lax.rem(p + size_p - 1, size_p), lax.rem(p + 1, size_p)

    def row_peer(d):
        k = lax.rem(x_hi * size_a + a + d, 2 * size_a)
        return (y * 2 + k // size_a, s, lax.rem(k, size_a))

    def plane_peer(d):
        dy, dz = d // 4, d % 4
        return (lax.rem(p + 2 * dy, size_p), lax.rem(s + dz, size_s), a)

    other = lax.rem(p - 1 + 2 * x_hi + size_p, size_p)
    bar = pltpu.get_barrier_semaphore()
    peers = [(other, s, a)]
    peers += [row_peer(d) for d in range(1, 8)]
    peers += [plane_peer(4 * d) for d in range(1, 4)]
    peers += [plane_peer(d) for d in range(1, 4)]
    for peer in peers:
        pl.semaphore_signal(bar, inc=1, device_id=peer, device_id_type=MESH)

    loads = [
        pltpu.make_async_copy(guess, st.at[0, :, :, :, pl.ds(8, 16), :], ld_sem.at[0]),
        pltpu.make_async_copy(diss_h, ds, ld_sem.at[1]),
        pltpu.make_async_copy(omega_h, om, ld_sem.at[2]),
        pltpu.make_async_copy(pseudo_h, ps, ld_sem.at[3]),
        pltpu.make_async_copy(right_h, rs, ld_sem.at[4]),
        pltpu.make_async_copy(diag_h, dg, ld_sem.at[5]),
    ] + [pltpu.make_async_copy(neigh_h.at[d], nb.at[d], ld_sem.at[6 + d]) for d in range(6)]
    for load in loads:
        load.start()

    rows_zero = jnp.zeros((2, 2, 6, 8, 2, 128), F32)
    ax_zero = jnp.zeros((2, 8, 8, 128), F32)

    @pl.when(s == 0)
    def _():
        st[:, :, :, :, 6:8, :] = rows_zero

    @pl.when(s == size_s - 1)
    def _():
        st[:, :, :, :, 24:26, :] = rows_zero

    @pl.when(a == 0)
    def _():
        axr[:, 0] = ax_zero

    @pl.when(a == size_a - 1)
    def _():
        axr[:, 1] = ax_zero

    sq[...] = jnp.zeros((2, 8, 128), F32)
    angle = jnp.full((8, 128), phase[0], F32)
    cosine, sine = jnp.cos(angle), jnp.sin(angle)
    first, last = p == 0, p == size_p - 1
    turn = (
        (jnp.where(first, cosine, 1.0), jnp.where(first, -sine, 0.0)),
        (jnp.where(last, cosine, 1.0), jnp.where(last, sine, 0.0)),
    )
    lane = lax.broadcasted_iota(jnp.int32, (8, 128), 1)
    lane16 = lax.broadcasted_iota(jnp.int32, (16, 128), 1)

    pl.semaphore_wait(bar, len(peers))

    def pitch_copy(it, way, t):
        layers = pl.ds(0, 2) if way == 0 else pl.ds(6, 2)
        if it == 0:
            src = guess.at[:, :, layers, pl.ds(8 * t, 8), :]
        else:
            src = st.at[1, :, :, layers, pl.ds(8 + 8 * t, 8), :]
        return pltpu.make_async_remote_copy(
            src_ref=src,
            dst_ref=hal.at[it, 1 - way, :, :, :, pl.ds(8 * t, 8), :],
            send_sem=psend.at[it, way, t],
            recv_sem=precv.at[it, 1 - way, t],
            device_id=(lower if way == 0 else upper, s, a),
            device_id_type=MESH,
        )

    groups = ((2, 4), (0, 2), (6, 2))

    def span_copy(it, way, group):
        first_layer, count = (0, 8) if it == 0 else groups[group]
        layers = pl.ds(first_layer, count)
        row = 0 if way == 0 else 14
        if it == 0:
            src = guess.at[:, :, layers, pl.ds(row, 2), :]
        else:
            src = st.at[1, :, :, layers, pl.ds(8 + row, 2), :]
        return pltpu.make_async_remote_copy(
            src_ref=src,
            dst_ref=st.at[it, :, :, layers, pl.ds(24 if way == 0 else 6, 2), :],
            send_sem=zsend.at[it, way, group],
            recv_sem=zrecv.at[it, 1 - way, group],
            device_id=(p, lax.rem(s + (size_s - 1 if way == 0 else 1), size_s), a),
            device_id_type=MESH,
        )

    def axial_copy(it, way, group):
        first_layer, count = (0, 8) if it == 0 else groups[group]
        return pltpu.make_async_remote_copy(
            src_ref=axs.at[it, pl.ds(first_layer, count)],
            dst_ref=axr.at[it, 1 - way, pl.ds(first_layer, count)],
            send_sem=asend.at[it, way, group],
            recv_sem=arecv.at[it, 1 - way, group],
            device_id=(p, s, lax.rem(a + (size_a - 1 if way == 0 else 1), size_a)),
            device_id_type=MESH,
        )

    has_span = (s > 0, s < size_s - 1)
    has_axial = (a > 0, a < size_a - 1)

    def span_start(it, way, group):
        @pl.when(has_span[way])
        def _():
            span_copy(it, way, group).start()

    def axial_start(it, group):
        for way in range(2):
            @pl.when(has_axial[way])
            def _():
                axial_copy(it, way, group).start()

    def side_wait(it, group):
        for way in range(2):
            @pl.when(has_span[way])
            def _():
                span_copy(it, 1 - way, group).wait_recv()

            @pl.when(has_axial[way])
            def _():
                axial_copy(it, 1 - way, group).wait_recv()

    def side_drain(it, group):
        for way in range(2):
            @pl.when(has_span[way])
            def _():
                span_copy(it, way, group).wait_send()

            @pl.when(has_axial[way])
            def _():
                axial_copy(it, way, group).wait_send()

    def pack(it, q):
        packed = jnp.zeros((8, 128), F32)
        for c in range(2):
            for v in range(6):
                for t in range(2):
                    k = (c * 6 + v) * 2 + t
                    tile = st[it, c, v, q, 8 + 8 * t : 16 + 8 * t, :]
                    packed = jnp.where(lane // 4 == k, pltpu.roll(tile, 4 * k + 2, 1), packed)
        axs[it, q] = packed

    def store(it, q, rows, c, residual, state):
        new = state + ps[q, rows, :][None] * residual
        if it == ITERS - 1:
            out[c, :, q, rows, :] = new
        else:
            st[1, c, :, q, pl.ds(8 + rows.start, rows.size), :] = new

    def add_square(it, residuals):
        total = sq[it]
        for residual in residuals:
            total = total + jnp.sum((residual * residual).reshape(-1, 8, 128), axis=0)
        sq[it] = total

    def partial(it, q, low, high, keep):
        acc = [None, None]

        def add(c, term):
            acc[c] = term if acc[c] is None else acc[c] + term

        centre = [st[it, c, :, q, 8:24, :] for c in range(2)]
        mixed = jnp.where(lax.rem(lane, 4) < 2, axr[it, 0, q], axr[it, 1, q])
        far = [[], []]
        for j in range(6):
            blocks = [dg[:, j, q], nb[2, :, j, q], nb[3, :, j, q], nb[4, :, j, q], nb[5, :, j, q]]
            if low >= 1:
                blocks.append(nb[0, :, j, q])
            if high >= 1:
                blocks.append(nb[1, :, j, q])
            blocks = [block.astype(F32) for block in blocks]
            for c in range(2):
                u = st[it, c, j, q, 8:24, :]
                k = (c * 6 + j) * 2
                rim = jnp.concatenate(
                    [pltpu.roll(mixed, (128 - 4 * (k + t) - 2) % 128, 1) for t in range(2)], axis=0
                )
                values = [
                    u,
                    st[it, c, j, q, 7:23, :],
                    st[it, c, j, q, 9:25, :],
                    pltpu.roll(jnp.where(lane16 == 127, rim, u), 1, 1),
                    pltpu.roll(jnp.where(lane16 == 0, rim, u), 127, 1),
                ]
                if low >= 1:
                    values.append(st[it, c, j, q - 1, 8:24, :])
                if high >= 1:
                    values.append(st[it, c, j, q + 1, 8:24, :])
                for block, value in zip(blocks, values):
                    add(c, block * value[None])
                far[c].append(
                    pltpu.roll(jnp.where(lane16 >= 126, rim, u), 2, 1)
                    + pltpu.roll(jnp.where(lane16 < 2, rim, u), 126, 1)
                )
        for c in range(2):
            if low == 2 and high == 2:
                add(c, ds[0, q][None] * (st[it, c, :, q - 2, 8:24, :] + st[it, c, :, q + 2, 8:24, :]))
            elif low == 2:
                add(c, ds[0, q][None] * st[it, c, :, q - 2, 8:24, :])
            else:
                add(c, ds[0, q][None] * st[it, c, :, q + 2, 8:24, :])
            add(c, ds[1, q][None] * (st[it, c, :, q, 6:22, :] + st[it, c, :, q, 10:26, :]))
            add(c, ds[2, q][None] * jnp.stack(far[c]))
        add(0, -(om[q][None] * centre[1]))
        add(1, om[q][None] * centre[0])
        residuals = [rs[c, :, q] - acc[c] for c in range(2)]
        if keep is not None:
            for c in range(2):
                prt[c, :, keep] = residuals[c]
        else:
            for c in range(2):
                store(it, q, pl.ds(0, 16), c, residuals[c], centre[c])
            add_square(it, residuals)

    def faces(it):
        partial(it, 0, 0, 2, 0)
        partial(it, 1, 1, 2, 1)
        partial(it, 6, 2, 1, 2)
        partial(it, 7, 2, 0, 3)

    def inner(it):
        def step(i, carry):
            partial(it, i + 2, 2, 2, None)
            return carry

        lax.fori_loop(0, 4, step, 0)

    def finish(it, face, t):
        rows = pl.ds(8 * t, 8)
        cos_v, sin_v = turn[face]
        near_at, far_at = (1, 0) if face == 0 else (0, 1)

        def rotated(at):
            real, imag = hal[it, face, 0, :, at, rows, :], hal[it, face, 1, :, at, rows, :]
            return [cos_v[None] * real - sin_v[None] * imag, sin_v[None] * real + cos_v[None] * imag]

        near, far = rotated(near_at), rotated(far_at)
        edge, second = (0, 1) if face == 0 else (7, 6)
        keep_edge, keep_second = (0, 1) if face == 0 else (3, 2)
        acc = [ds[0, edge, rows, :][None] * far[c] for c in range(2)]
        for j in range(6):
            block = nb[face, :, j, edge, rows, :].astype(F32)
            for c in range(2):
                acc[c] = acc[c] + block * near[c][j][None]
        squares = []
        for c in range(2):
            residual = prt[c, :, keep_edge, rows, :] - acc[c]
            squares.append(residual)
            store(it, edge, rows, c, residual, st[it, c, :, edge, 8 + 8 * t : 16 + 8 * t, :])
            residual = prt[c, :, keep_second, rows, :] - ds[0, second, rows, :][None] * near[c]
            squares.append(residual)
            store(it, second, rows, c, residual, st[it, c, :, second, 8 + 8 * t : 16 + 8 * t, :])
        add_square(it, squares)

    for t in range(2):
        for way in range(2):
            pitch_copy(0, way, t).start()
    for way in range(2):
        span_start(0, way, 0)
    for d in range(1, 4):
        pl.semaphore_signal(ready, inc=1, device_id=plane_peer(d), device_id_type=MESH)
    loads[0].wait()

    def pack_step(it, base):
        def step(i, carry):
            pack(it, i + base)
            return carry

        return step

    lax.fori_loop(0, 8, pack_step(0, 0), 0)
    axial_start(0, 0)
    for load in loads[1:]:
        load.wait()
    side_wait(0, 0)
    faces(0)
    inner(0)
    for way in range(2):
        span_start(1, way, 0)
    lax.fori_loop(0, 4, pack_step(1, 2), 0)
    axial_start(1, 0)
    for t in range(2):
        for face in range(2):
            pitch_copy(0, 1 - face, t).wait_recv()
            finish(0, face, t)
            pitch_copy(1, face, t).start()
            span_start(1, t, 1 + face)
    lax.fori_loop(0, 2, pack_step(1, 0), 0)
    axial_start(1, 1)
    lax.fori_loop(0, 2, pack_step(1, 6), 0)
    axial_start(1, 2)

    side_wait(1, 0)
    inner(1)
    side_wait(1, 1)
    side_wait(1, 2)
    faces(1)
    for t in range(2):
        for face in range(2):
            pitch_copy(1, 1 - face, t).wait_recv()
            finish(1, face, t)

    half = lax.broadcasted_iota(jnp.int32, (1, 128), 1) < 64

    def folded(it):
        row = jnp.sum(sq[it], axis=0, keepdims=True)
        return row + pltpu.roll(row, 64, 1)

    total = jnp.where(half, folded(0), folded(1))
    row_index, plane_index = x_hi * size_a + a, y * size_s + s
    for stage in range(2):
        count = (8, 16)[stage]
        base = (0, 8)[stage]
        mine = base + (row_index, plane_index)[stage]
        peer_of = (row_peer, plane_peer)[stage]
        tot_s[pl.ds(8 * stage, 1)] = total
        if stage == 1:
            pl.semaphore_wait(ready, 3)
        for d in range(1, count):
            pltpu.make_async_remote_copy(
                src_ref=tot_s.at[pl.ds(8 * stage, 1)],
                dst_ref=red.at[pl.ds(mine, 1)],
                send_sem=rsend.at[stage],
                recv_sem=rrecv.at[stage],
                device_id=peer_of(d),
                device_id_type=MESH,
            ).start()
        got = red.at[pl.ds(base, count - 1)]
        pltpu.make_async_copy(got, got, rrecv.at[stage]).wait()
        rows = red[base : base + count]
        index = lax.broadcasted_iota(jnp.int32, (count, 128), 0) + base
        total = total + jnp.sum(jnp.where(index == mine, 0.0, rows), axis=0, keepdims=True)
    first_sum = jnp.sum(jnp.where(half, total, 0.0), axis=1, keepdims=True)
    second_sum = jnp.sum(jnp.where(half, 0.0, total), axis=1, keepdims=True)
    cells = float(12 * 8 * 16 * 128) * (size_p * size_s * size_a)
    lane1 = lax.broadcasted_iota(jnp.int32, (1, 128), 1)
    norms[...] = jnp.sqrt(jnp.where(lane1 == 0, first_sum, second_sum) / cells)

    for it in range(2):
        for t in range(2):
            for way in range(2):
                pitch_copy(it, way, t).wait_send()
        for group in range(1 if it == 0 else 3):
            side_drain(it, group)
    for stage in range(2):
        count = (8, 16)[stage]
        sent = red.at[pl.ds((0, 8)[stage], count - 1)]
        pltpu.make_async_copy(sent, sent, rsend.at[stage]).wait()


def body(guess, right_side, diag_block, neighbour_blocks, dissipation, omega_volume, pseudo_step, phase):
    anywhere = pl.BlockSpec(memory_space=pl.ANY)
    dma = pltpu.SemaphoreType.DMA
    field, norms = pl.pallas_call(
        kernel,
        out_shape=(
            jax.ShapeDtypeStruct(guess.shape, F32),
            jax.ShapeDtypeStruct((1, 128), F32),
        ),
        in_specs=[anywhere] * 7 + [pl.BlockSpec(memory_space=pltpu.SMEM)],
        out_specs=(
            pl.BlockSpec(memory_space=pltpu.VMEM),
            pl.BlockSpec(memory_space=pltpu.VMEM),
        ),
        scratch_shapes=[
            pltpu.VMEM((2, 2, 6, 8, 32, 128), F32),
            pltpu.VMEM((2, 2, 2, 6, 2, 16, 128), F32),
            pltpu.VMEM((2, 6, 4, 16, 128), F32),
            pltpu.VMEM((2, 6, 8, 16, 128), F32),
            pltpu.VMEM((6, 6, 8, 16, 128), jnp.bfloat16),
            pltpu.VMEM((6, 6, 6, 8, 16, 128), jnp.bfloat16),
            pltpu.VMEM((3, 8, 16, 128), F32),
            pltpu.VMEM((8, 16, 128), F32),
            pltpu.VMEM((8, 16, 128), F32),
            pltpu.VMEM((2, 8, 8, 128), F32),
            pltpu.VMEM((2, 2, 8, 8, 128), F32),
            pltpu.VMEM((2, 8, 128), F32),
            pltpu.VMEM((24, 128), F32),
            pltpu.VMEM((16, 128), F32),
            dma((12,)),
            dma((2, 2, 2)),
            dma((2, 2, 2)),
            dma((2, 2, 3)),
            dma((2, 2, 3)),
            dma((2, 2, 3)),
            dma((2, 2, 3)),
            dma((2,)),
            dma((2,)),
            pltpu.SemaphoreType.REGULAR,
        ],
        compiler_params=pltpu.CompilerParams(
            collective_id=0, has_side_effects=True, vmem_limit_bytes=40 * 1024 * 1024
        ),
        name="tangent",
    )(guess, right_side, diag_block, neighbour_blocks, dissipation, omega_volume, pseudo_step, phase)
    return field, norms[0, :2]


def solution(mesh):
    placed = (
        P(None, None, "pitch", "span", "axial"),
        P(None, None, "pitch", "span", "axial"),
        P(None, None, "pitch", "span", "axial"),
        P(None, None, None, "pitch", "span", "axial"),
        P(None, "pitch", "span", "axial"),
        P("pitch", "span", "axial"),
        P("pitch", "span", "axial"),
        P(),
    )
    return jax.shard_map(
        body,
        mesh=mesh,
        in_specs=placed,
        out_specs=(P(None, None, "pitch", "span", "axial"), P()),
        check_vma=False,
    )
```

```python
import functools

import jax
import jax.numpy as jnp
from jax import lax
from jax.experimental import pallas as pl
from jax.experimental.pallas import tpu as pltpu
from jax.sharding import PartitionSpec as P

ITERS = 2
MESH = pl.DeviceIdType.MESH
F32 = jnp.float32


def kernel(
    guess, right_h, diag_h, neigh_h, diss_h, omega_h, pseudo_h, phase_h,
    out, norms,
    st, hal, prt, rs, dg, nb, ds, om, ps, axs, axr, sq, red, tot_s, phase,
    ld_sem, psend, precv, zsend, zrecv, asend, arecv, rsend, rrecv, ready,
):
    p, s, a = lax.axis_index("pitch"), lax.axis_index("span"), lax.axis_index("axial")
    size_p, size_s, size_a = lax.axis_size("pitch"), lax.axis_size("span"), lax.axis_size("axial")
    y, x_hi = p // 2, lax.rem(p, 2)

    def row_peer(d):
        k = lax.rem(x_hi * size_a + a + d, 2 * size_a)
        return (y * 2 + k // size_a, s, lax.rem(k, size_a))

    def plane_peer(d):
        dy, dz = d // 4, d % 4
        return (lax.rem(p + 2 * dy, size_p), lax.rem(s + dz, size_s), a)

    other = lax.rem(p - 1 + 2 * x_hi + size_p, size_p)
    bar = pltpu.get_barrier_semaphore()
    peers = [(other, s, a)]
    peers += [row_peer(d) for d in range(1, 8)]
    peers += [plane_peer(4 * d) for d in range(1, 4)]
    peers += [plane_peer(d) for d in range(1, 4)]
    for peer in peers:
        pl.semaphore_signal(bar, inc=1, device_id=peer, device_id_type=MESH)

    loads = [
        pltpu.make_async_copy(guess, st.at[0, :, :, pl.ds(2, 8), pl.ds(8, 16), :], ld_sem.at[0]),
        pltpu.make_async_copy(diss_h, ds, ld_sem.at[1]),
        pltpu.make_async_copy(omega_h, om, ld_sem.at[2]),
        pltpu.make_async_copy(pseudo_h, ps, ld_sem.at[3]),
        pltpu.make_async_copy(right_h, rs, ld_sem.at[4]),
        pltpu.make_async_copy(diag_h, dg, ld_sem.at[5]),
    ] + [pltpu.make_async_copy(neigh_h.at[d], nb.at[d], ld_sem.at[6 + d]) for d in range(6)]
    phase_load = pltpu.make_async_copy(phase_h, phase, ld_sem.at[12])
    phase_load.start()
    for load in loads:
        load.start()

    rows_zero = jnp.zeros((2, 2, 6, 8, 2, 128), F32)
    ax_zero = jnp.zeros((2, 8, 8, 128), F32)
    layers_zero = jnp.zeros((2, 2, 6, 2, 16, 128), F32)
    st[:, :, :, 0:2, 8:24, :] = layers_zero
    st[:, :, :, 10:12, 8:24, :] = layers_zero

    @pl.when(s == 0)
    def _():
        st[:, :, :, 2:10, 6:8, :] = rows_zero

    @pl.when(s == size_s - 1)
    def _():
        st[:, :, :, 2:10, 24:26, :] = rows_zero

    @pl.when(a == 0)
    def _():
        axr[:, 0] = ax_zero

    @pl.when(a == size_a - 1)
    def _():
        axr[:, 1] = ax_zero

    sq[...] = jnp.zeros((2, 8, 128), F32)
    phase_load.wait()
    angle = jnp.full((8, 128), phase[0], F32)
    cosine, sine = jnp.cos(angle), jnp.sin(angle)
    first, last = p == 0, p == size_p - 1
    turn_cos = jnp.where(first | last, cosine, 1.0)
    turn_sin = jnp.where(first, -sine, jnp.where(last, sine, 0.0))
    lane = lax.broadcasted_iota(jnp.int32, (8, 128), 1)
    lane16 = lax.broadcasted_iota(jnp.int32, (16, 128), 1)
    faces = (x_hi, 1 - x_hi)
    OTHER, SAME = 0, 1

    pl.semaphore_wait(bar, len(peers))

    def pitch_copy(it, kind, t):
        face = faces[kind]
        layers = pl.ds(6 * face, 2)
        if it == 0:
            src = guess.at[:, :, layers, pl.ds(8 * t, 8), :]
        else:
            src = st.at[1, :, :, pl.ds(2 + 6 * face, 2), pl.ds(8 + 8 * t, 8), :]
        return pltpu.make_async_remote_copy(
            src_ref=src,
            dst_ref=hal.at[it, kind, :, :, :, pl.ds(8 * t, 8), :],
            send_sem=psend.at[it, kind, t],
            recv_sem=precv.at[it, kind, t],
            device_id=(lax.rem(p + size_p - 1 + 2 * face, size_p), s, a),
            device_id_type=MESH,
        )

    INNER = 2
    groups = ((6 * faces[0], 2), (6 * faces[1], 2), (2, 4))

    def span_copy(it, way, group):
        first_layer, count = (0, 8) if it == 0 else groups[group]
        row = 0 if way == 0 else 14
        if it == 0:
            src = guess.at[:, :, pl.ds(first_layer, count), pl.ds(row, 2), :]
        else:
            src = st.at[1, :, :, pl.ds(2 + first_layer, count), pl.ds(8 + row, 2), :]
        return pltpu.make_async_remote_copy(
            src_ref=src,
            dst_ref=st.at[it, :, :, pl.ds(2 + first_layer, count), pl.ds(24 if way == 0 else 6, 2), :],
            send_sem=zsend.at[it, way, group],
            recv_sem=zrecv.at[it, 1 - way, group],
            device_id=(p, lax.rem(s + (size_s - 1 if way == 0 else 1), size_s), a),
            device_id_type=MESH,
        )

    def axial_copy(it, way, group):
        first_layer, count = (0, 8) if it == 0 else groups[group]
        return pltpu.make_async_remote_copy(
            src_ref=axs.at[it, pl.ds(first_layer, count)],
            dst_ref=axr.at[it, 1 - way, pl.ds(first_layer, count)],
            send_sem=asend.at[it, way, group],
            recv_sem=arecv.at[it, 1 - way, group],
            device_id=(p, s, lax.rem(a + (size_a - 1 if way == 0 else 1), size_a)),
            device_id_type=MESH,
        )

    has_span = (s > 0, s < size_s - 1)
    has_axial = (a > 0, a < size_a - 1)

    def span_start(it, way, group):
        @pl.when(has_span[way])
        def _():
            span_copy(it, way, group).start()

    def axial_start(it, group):
        for way in range(2):
            @pl.when(has_axial[way])
            def _():
                axial_copy(it, way, group).start()

    def side_wait(it, group):
        for way in range(2):
            @pl.when(has_span[way])
            def _():
                span_copy(it, 1 - way, group).wait_recv()

            @pl.when(has_axial[way])
            def _():
                axial_copy(it, 1 - way, group).wait_recv()

    def side_drain(it, group):
        for way in range(2):
            @pl.when(has_span[way])
            def _():
                span_copy(it, way, group).wait_send()

            @pl.when(has_axial[way])
            def _():
                axial_copy(it, way, group).wait_send()

    def over(count, layer_of, work):
        def step(i, carry):
            work(layer_of(i))
            return carry

        lax.fori_loop(0, count, step, 0)

    def pack(it, q):
        packed = jnp.zeros((8, 128), F32)
        for c in range(2):
            for v in range(6):
                for t in range(2):
                    k = (c * 6 + v) * 2 + t
                    tile = st[it, c, v, q + 2, 8 + 8 * t : 16 + 8 * t, :]
                    packed = jnp.where(lane // 4 == k, pltpu.roll(tile, 4 * k + 2, 1), packed)
        axs[it, q] = packed

    def store(it, q, rows, c, v, residual, state):
        new = state + ps[q, rows, :] * residual
        if it == ITERS - 1:
            out[c, v, q, rows, :] = new
        else:
            st[1, c, v, q + 2, pl.ds(8 + rows.start, rows.size), :] = new

    def add_square(it, residuals):
        total = sq[it]
        for residual in residuals:
            square = residual * residual
            for t in range(residual.shape[0] // 8):
                total = total + square[8 * t : 8 * t + 8]
        sq[it] = total

    def times(left, block_of, values):
        for i in range(6):
            block = block_of(i).astype(F32)
            for c in range(2):
                left[c][i] = left[c][i] - block * values[c]

    def own_terms(it, q):
        left = [[rs[c, i, q] for i in range(6)] for c in range(2)]
        for j in range(6):
            times(left, lambda i: dg[i, j, q], [st[it, c, j, q + 2, 8:24, :] for c in range(2)])
        for d in range(2):
            for j in range(6):
                times(left, lambda i: nb[d, i, j, q], [st[it, c, j, q + 1 + 2 * d, 8:24, :] for c in range(2)])
        for i in range(6):
            for c in range(2):
                value = left[c][i]
                value = value - ds[0, q] * (st[it, c, i, q, 8:24, :] + st[it, c, i, q + 4, 8:24, :])
                turned = om[q] * st[it, 1 - c, i, q + 2, 8:24, :]
                prt[c, i, q] = value + turned if c == 0 else value - turned

    def side_terms(it, q, keep):
        left = [[prt[c, i, q] for i in range(6)] for c in range(2)]
        for d in range(2):
            for j in range(6):
                times(left, lambda i: nb[2 + d, i, j, q], [st[it, c, j, q + 2, 7 + 2 * d : 23 + 2 * d, :] for c in range(2)])
        mixed = jnp.where(lax.rem(lane, 4) < 2, axr[it, 0, q], axr[it, 1, q])
        for j in range(6):
            below, above = [], []
            for c in range(2):
                u = st[it, c, j, q + 2, 8:24, :]
                k = (c * 6 + j) * 2
                rim = jnp.concatenate([pltpu.roll(mixed, 126 - 4 * (k + t), 1) for t in range(2)], axis=0)
                below.append(pltpu.roll(jnp.where(lane16 == 127, rim, u), 1, 1))
                above.append(pltpu.roll(jnp.where(lane16 == 0, rim, u), 127, 1))
                left[c][j] = left[c][j] - ds[2, q] * (
                    pltpu.roll(jnp.where(lane16 >= 126, rim, u), 2, 1)
                    + pltpu.roll(jnp.where(lane16 < 2, rim, u), 126, 1)
                )
            times(left, lambda i: nb[4, i, j, q], below)
            times(left, lambda i: nb[5, i, j, q], above)
        for i in range(6):
            for c in range(2):
                left[c][i] = left[c][i] - ds[1, q] * (
                    st[it, c, i, q + 2, 6:22, :] + st[it, c, i, q + 2, 10:26, :]
                )
                if keep:
                    prt[c, i, q] = left[c][i]
                else:
                    store(it, q, pl.ds(0, 16), c, i, left[c][i], st[it, c, i, q + 2, 8:24, :])
        if not keep:
            add_square(it, left[0] + left[1])

    def finish(it, kind, t):
        rows = pl.ds(8 * t, 8)
        body_rows = pl.ds(8 + 8 * t, 8)
        face = faces[kind]

        def rim(at):
            real = [hal[it, kind, 0, j, at, rows, :] for j in range(6)]
            imag = [hal[it, kind, 1, j, at, rows, :] for j in range(6)]
            if kind == SAME:
                return [real, imag]
            return [
                [turn_cos * x - turn_sin * w for x, w in zip(real, imag)],
                [turn_sin * x + turn_cos * w for x, w in zip(real, imag)],
            ]

        near, far = rim(1 - face), rim(face)
        edge, second = 7 * face, 1 + 5 * face
        left = [[prt[c, i, edge, rows, :] for i in range(6)] for c in range(2)]
        for j in range(6):
            times(left, lambda i: nb[face, i, j, edge, rows, :], [near[c][j] for c in range(2)])
        squares = []
        for c in range(2):
            for i in range(6):
                residual = left[c][i] - ds[0, edge, rows, :] * far[c][i]
                squares.append(residual)
                store(it, edge, rows, c, i, residual, st[it, c, i, edge + 2, body_rows, :])
                residual = prt[c, i, second, rows, :] - ds[0, second, rows, :] * near[c][i]
                squares.append(residual)
                store(it, second, rows, c, i, residual, st[it, c, i, second + 2, body_rows, :])
        add_square(it, squares)

    every = (8, lambda i: i)
    inner = (4, lambda i: i + 2)
    outer = (4, lambda i: i + 4 * (i // 2))
    order = ((0, OTHER), (0, SAME), (1, OTHER), (1, SAME))

    for way in range(2):
        span_start(0, way, 0)
    for t, kind in order:
        pitch_copy(0, kind, t).start()
    for d in range(1, 4):
        pl.semaphore_signal(ready, inc=1, device_id=plane_peer(d), device_id_type=MESH)
    loads[0].wait()
    over(*every, lambda q: pack(0, q))
    axial_start(0, 0)
    for load in loads[1:]:
        load.wait()
    over(*every, lambda q: own_terms(0, q))
    side_wait(0, 0)
    over(*outer, lambda q: side_terms(0, q, True))
    over(*inner, lambda q: side_terms(0, q, False))
    for way in range(2):
        span_start(1, way, INNER)
    over(*inner, lambda q: pack(1, q))
    axial_start(1, INNER)
    for t, kind in order:
        pitch_copy(0, kind, t).wait_recv()
        finish(0, kind, t)
        pitch_copy(1, kind, t).start()
        span_start(1, t, kind)
    over(*outer, lambda q: pack(1, q))
    for kind in range(2):
        axial_start(1, kind)

    over(*every, lambda q: own_terms(1, q))
    side_wait(1, INNER)
    over(*inner, lambda q: side_terms(1, q, False))
    for kind in range(2):
        side_wait(1, kind)
    over(*outer, lambda q: side_terms(1, q, True))
    for t, kind in order:
        pitch_copy(1, kind, t).wait_recv()
        finish(1, kind, t)

    half = lax.broadcasted_iota(jnp.int32, (1, 128), 1) < 64

    def folded(it):
        row = jnp.sum(sq[it], axis=0, keepdims=True)
        return row + pltpu.roll(row, 64, 1)

    total = jnp.where(half, folded(0), folded(1))
    row_index, plane_index = x_hi * size_a + a, y * size_s + s
    for stage in range(2):
        count = (8, 16)[stage]
        base = (0, 8)[stage]
        mine = base + (row_index, plane_index)[stage]
        peer_of = (row_peer, plane_peer)[stage]
        tot_s[pl.ds(8 * stage, 1)] = total
        if stage == 1:
            pl.semaphore_wait(ready, 3)
        for d in range(1, count):
            pltpu.make_async_remote_copy(
                src_ref=tot_s.at[pl.ds(8 * stage, 1)],
                dst_ref=red.at[pl.ds(mine, 1)],
                send_sem=rsend.at[stage],
                recv_sem=rrecv.at[stage],
                device_id=peer_of(d),
                device_id_type=MESH,
            ).start()
        got = red.at[pl.ds(base, count - 1)]
        pltpu.make_async_copy(got, got, rrecv.at[stage]).wait()
        rows = red[base : base + count]
        index = lax.broadcasted_iota(jnp.int32, (count, 128), 0) + base
        total = total + jnp.sum(jnp.where(index == mine, 0.0, rows), axis=0, keepdims=True)
    first_sum = jnp.sum(jnp.where(half, total, 0.0), axis=1, keepdims=True)
    second_sum = jnp.sum(jnp.where(half, 0.0, total), axis=1, keepdims=True)
    cells = float(12 * 8 * 16 * 128) * (size_p * size_s * size_a)
    lane1 = lax.broadcasted_iota(jnp.int32, (1, 128), 1)
    norms[...] = jnp.sqrt(jnp.where(lane1 == 0, first_sum, second_sum) / cells)

    for it in range(2):
        for t in range(2):
            for kind in range(2):
                pitch_copy(it, kind, t).wait_send()
        for group in range(1 if it == 0 else 3):
            side_drain(it, group)
    for stage in range(2):
        count = (8, 16)[stage]
        sent = red.at[pl.ds((0, 8)[stage], count - 1)]
        pltpu.make_async_copy(sent, sent, rsend.at[stage]).wait()


def body(guess, right_side, diag_block, neighbour_blocks, dissipation, omega_volume, pseudo_step, phase):
    anywhere = pl.BlockSpec(memory_space=pltpu.HBM)
    dma = pltpu.SemaphoreType.DMA
    field, norms = pl.pallas_call(
        kernel,
        out_shape=(
            jax.ShapeDtypeStruct(guess.shape, F32),
            jax.ShapeDtypeStruct((1, 128), F32),
        ),
        in_specs=[anywhere] * 8,
        out_specs=(pl.BlockSpec(memory_space=pltpu.VMEM), pl.BlockSpec(memory_space=pltpu.VMEM)),
        scratch_shapes=[
            pltpu.VMEM((2, 2, 6, 12, 32, 128), F32),
            pltpu.VMEM((2, 2, 2, 6, 2, 16, 128), F32),
            pltpu.VMEM((2, 6, 8, 16, 128), F32),
            pltpu.VMEM((2, 6, 8, 16, 128), F32),
            pltpu.VMEM((6, 6, 8, 16, 128), jnp.bfloat16),
            pltpu.VMEM((6, 6, 6, 8, 16, 128), jnp.bfloat16),
            pltpu.VMEM((3, 8, 16, 128), F32),
            pltpu.VMEM((8, 16, 128), F32),
            pltpu.VMEM((8, 16, 128), F32),
            pltpu.VMEM((2, 8, 8, 128), F32),
            pltpu.VMEM((2, 2, 8, 8, 128), F32),
            pltpu.VMEM((2, 8, 128), F32),
            pltpu.VMEM((24, 128), F32),
            pltpu.VMEM((16, 128), F32),
            pltpu.SMEM((1,), F32),
            dma((14,)),
            dma((2, 2, 2)),
            dma((2, 2, 2)),
            dma((2, 2, 3)),
            dma((2, 2, 3)),
            dma((2, 2, 3)),
            dma((2, 2, 3)),
            dma((2,)),
            dma((2,)),
            pltpu.SemaphoreType.REGULAR,
        ],
        compiler_params=pltpu.CompilerParams(
            collective_id=0, has_side_effects=True, vmem_limit_bytes=40 * 1024 * 1024
        ),
        name="tangent",
    )(*(
        pltpu.with_memory_space_constraint(operand, pltpu.HBM)
        for operand in (
            guess, right_side, diag_block, neighbour_blocks, dissipation, omega_volume, pseudo_step
        )
    ), phase)
    return field, norms[0, :2]


def solution(mesh):
    placed = (
        P(None, None, "pitch", "span", "axial"),
        P(None, None, "pitch", "span", "axial"),
        P(None, None, "pitch", "span", "axial"),
        P(None, None, None, "pitch", "span", "axial"),
        P(None, "pitch", "span", "axial"),
        P("pitch", "span", "axial"),
        P("pitch", "span", "axial"),
        P(),
    )
    return jax.shard_map(
        body,
        mesh=mesh,
        in_specs=placed,
        out_specs=(P(None, None, "pitch", "span", "axial"), P()),
        check_vma=False,
    )
```

```python
import functools

import jax
import jax.numpy as jnp
from jax import lax
from jax.experimental import pallas as pl
from jax.experimental.pallas import tpu as pltpu
from jax.sharding import PartitionSpec as P

ITERS = 2
MESH = pl.DeviceIdType.MESH
F32 = jnp.float32


def kernel(
    guess, right_h, diag_h, neigh_h, diss_h, omega_h, pseudo_h, phase_h,
    out, norms,
    st, hal, prt, rs, dg, nb, ds, om, ps, axs, axr, sq, red, tot_s, phase,
    ld_sem, psend, precv, zsend, zrecv, asend, arecv, rsend, rrecv, ready, ready_row,
):
    p, s, a = lax.axis_index("pitch"), lax.axis_index("span"), lax.axis_index("axial")
    size_p, size_s, size_a = lax.axis_size("pitch"), lax.axis_size("span"), lax.axis_size("axial")
    y, x_hi = p // 2, lax.rem(p, 2)

    def row_peer(d):
        k = lax.rem(x_hi * size_a + a + d, 2 * size_a)
        return (y * 2 + k // size_a, s, lax.rem(k, size_a))

    def plane_peer(d):
        dy, dz = d // 4, d % 4
        return (lax.rem(p + 2 * dy, size_p), lax.rem(s + dz, size_s), a)

    other = lax.rem(p - 1 + 2 * x_hi + size_p, size_p)
    bar = pltpu.get_barrier_semaphore()
    peers = [(other, s, a)]
    peers += [row_peer(d) for d in range(1, 8)]
    peers += [plane_peer(4 * d) for d in range(1, 4)]
    peers += [plane_peer(d) for d in range(1, 4)]
    for peer in peers:
        pl.semaphore_signal(bar, inc=1, device_id=peer, device_id_type=MESH)

    loads = [
        pltpu.make_async_copy(guess, st.at[0, :, :, pl.ds(2, 8), pl.ds(8, 16), :], ld_sem.at[0]),
        pltpu.make_async_copy(diss_h, ds, ld_sem.at[1]),
        pltpu.make_async_copy(omega_h, om, ld_sem.at[2]),
        pltpu.make_async_copy(pseudo_h, ps, ld_sem.at[3]),
        pltpu.make_async_copy(right_h, rs, ld_sem.at[4]),
        pltpu.make_async_copy(diag_h, dg, ld_sem.at[5]),
    ] + [pltpu.make_async_copy(neigh_h.at[d], nb.at[d], ld_sem.at[6 + d]) for d in range(6)]
    phase_load = pltpu.make_async_copy(phase_h, phase, ld_sem.at[12])
    phase_load.start()
    for load in loads:
        load.start()

    rows_zero = jnp.zeros((2, 2, 6, 8, 2, 128), F32)
    ax_zero = jnp.zeros((2, 8, 8, 128), F32)
    layers_zero = jnp.zeros((2, 2, 6, 2, 16, 128), F32)
    st[:, :, :, 0:2, 8:24, :] = layers_zero
    st[:, :, :, 10:12, 8:24, :] = layers_zero

    @pl.when(s == 0)
    def _():
        st[:, :, :, 2:10, 6:8, :] = rows_zero

    @pl.when(s == size_s - 1)
    def _():
        st[:, :, :, 2:10, 24:26, :] = rows_zero

    @pl.when(a == 0)
    def _():
        axr[:, 0] = ax_zero

    @pl.when(a == size_a - 1)
    def _():
        axr[:, 1] = ax_zero

    sq[...] = jnp.zeros((2, 8, 128), F32)
    phase_load.wait()
    angle = jnp.full((8, 128), phase[0], F32)
    cosine, sine = jnp.cos(angle), jnp.sin(angle)
    first, last = p == 0, p == size_p - 1
    turn_cos = jnp.where(first | last, cosine, 1.0)
    turn_sin = jnp.where(first, -sine, jnp.where(last, sine, 0.0))
    lane = lax.broadcasted_iota(jnp.int32, (8, 128), 1)
    lane16 = lax.broadcasted_iota(jnp.int32, (16, 128), 1)
    faces = (x_hi, 1 - x_hi)
    OTHER, SAME = 0, 1

    pl.semaphore_wait(bar, len(peers))

    def pitch_copy(it, kind, t):
        face = faces[kind]
        layers = pl.ds(6 * face, 2)
        if it == 0:
            src = guess.at[:, :, layers, pl.ds(8 * t, 8), :]
        else:
            src = st.at[1, :, :, pl.ds(2 + 6 * face, 2), pl.ds(8 + 8 * t, 8), :]
        return pltpu.make_async_remote_copy(
            src_ref=src,
            dst_ref=hal.at[it, kind, :, :, :, pl.ds(8 * t, 8), :],
            send_sem=psend.at[it, kind, t],
            recv_sem=precv.at[it, kind, t],
            device_id=(lax.rem(p + size_p - 1 + 2 * face, size_p), s, a),
            device_id_type=MESH,
        )

    INNER = 2
    groups = ((6 * faces[0], 2), (6 * faces[1], 2), (2, 4))

    def span_copy(it, way, group):
        first_layer, count = (0, 8) if it == 0 else groups[group]
        row = 0 if way == 0 else 14
        if it == 0:
            src = guess.at[:, :, pl.ds(first_layer, count), pl.ds(row, 2), :]
        else:
            src = st.at[1, :, :, pl.ds(2 + first_layer, count), pl.ds(8 + row, 2), :]
        return pltpu.make_async_remote_copy(
            src_ref=src,
            dst_ref=st.at[it, :, :, pl.ds(2 + first_layer, count), pl.ds(24 if way == 0 else 6, 2), :],
            send_sem=zsend.at[it, way, group],
            recv_sem=zrecv.at[it, 1 - way, group],
            device_id=(p, lax.rem(s + (size_s - 1 if way == 0 else 1), size_s), a),
            device_id_type=MESH,
        )

    def axial_copy(it, way, group):
        first_layer, count = (0, 8) if it == 0 else groups[group]
        return pltpu.make_async_remote_copy(
            src_ref=axs.at[it, pl.ds(first_layer, count)],
            dst_ref=axr.at[it, 1 - way, pl.ds(first_layer, count)],
            send_sem=asend.at[it, way, group],
            recv_sem=arecv.at[it, 1 - way, group],
            device_id=(p, s, lax.rem(a + (size_a - 1 if way == 0 else 1), size_a)),
            device_id_type=MESH,
        )

    has_span = (s > 0, s < size_s - 1)
    has_axial = (a > 0, a < size_a - 1)

    def span_start(it, way, group):
        @pl.when(has_span[way])
        def _():
            span_copy(it, way, group).start()

    def axial_start(it, group):
        for way in range(2):
            @pl.when(has_axial[way])
            def _():
                axial_copy(it, way, group).start()

    def side_wait(it, group):
        for way in range(2):
            @pl.when(has_span[way])
            def _():
                span_copy(it, 1 - way, group).wait_recv()

            @pl.when(has_axial[way])
            def _():
                axial_copy(it, 1 - way, group).wait_recv()

    def side_drain(it, group):
        for way in range(2):
            @pl.when(has_span[way])
            def _():
                span_copy(it, way, group).wait_send()

            @pl.when(has_axial[way])
            def _():
                axial_copy(it, way, group).wait_send()

    def over(count, layer_of, work):
        def step(i, carry):
            work(layer_of(i))
            return carry

        lax.fori_loop(0, count, step, 0)

    def pack(it, q):
        packed = jnp.zeros((8, 128), F32)
        for c in range(2):
            for v in range(6):
                for t in range(2):
                    k = (c * 6 + v) * 2 + t
                    tile = st[it, c, v, q + 2, 8 + 8 * t : 16 + 8 * t, :]
                    packed = jnp.where(lane // 4 == k, pltpu.roll(tile, 4 * k + 2, 1), packed)
        axs[it, q] = packed

    def store(it, q, rows, c, v, residual, state):
        new = state + ps[q, rows, :] * residual
        if it == ITERS - 1:
            out[c, v, q, rows, :] = new
        else:
            st[1, c, v, q + 2, pl.ds(8 + rows.start, rows.size), :] = new

    def add_square(it, residuals):
        total = sq[it]
        for residual in residuals:
            square = residual * residual
            for t in range(residual.shape[0] // 8):
                total = total + square[8 * t : 8 * t + 8]
        sq[it] = total

    def times(left, block_of, values):
        for i in range(6):
            block = block_of(i).astype(F32)
            for c in range(2):
                left[c][i] = left[c][i] - block * values[c]

    def own_terms(it, q):
        left = [[rs[c, i, q] for i in range(6)] for c in range(2)]
        for j in range(6):
            times(left, lambda i: dg[i, j, q], [st[it, c, j, q + 2, 8:24, :] for c in range(2)])
        for d in range(2):
            for j in range(6):
                times(left, lambda i: nb[d, i, j, q], [st[it, c, j, q + 1 + 2 * d, 8:24, :] for c in range(2)])
        for i in range(6):
            for c in range(2):
                value = left[c][i]
                value = value - ds[0, q] * (st[it, c, i, q, 8:24, :] + st[it, c, i, q + 4, 8:24, :])
                turned = om[q] * st[it, 1 - c, i, q + 2, 8:24, :]
                prt[c, i, q] = value + turned if c == 0 else value - turned

    def side_terms(it, q, keep):
        left = [[prt[c, i, q] for i in range(6)] for c in range(2)]
        for d in range(2):
            for j in range(6):
                times(left, lambda i: nb[2 + d, i, j, q], [st[it, c, j, q + 2, 7 + 2 * d : 23 + 2 * d, :] for c in range(2)])
        mixed = jnp.where(lax.rem(lane, 4) < 2, axr[it, 0, q], axr[it, 1, q])
        for j in range(6):
            below, above = [], []
            for c in range(2):
                u = st[it, c, j, q + 2, 8:24, :]
                k = (c * 6 + j) * 2
                rim = jnp.concatenate([pltpu.roll(mixed, 126 - 4 * (k + t), 1) for t in range(2)], axis=0)
                below.append(pltpu.roll(jnp.where(lane16 == 127, rim, u), 1, 1))
                above.append(pltpu.roll(jnp.where(lane16 == 0, rim, u), 127, 1))
                left[c][j] = left[c][j] - ds[2, q] * (
                    pltpu.roll(jnp.where(lane16 >= 126, rim, u), 2, 1)
                    + pltpu.roll(jnp.where(lane16 < 2, rim, u), 126, 1)
                )
            times(left, lambda i: nb[4, i, j, q], below)
            times(left, lambda i: nb[5, i, j, q], above)
        for i in range(6):
            for c in range(2):
                left[c][i] = left[c][i] - ds[1, q] * (
                    st[it, c, i, q + 2, 6:22, :] + st[it, c, i, q + 2, 10:26, :]
                )
                if keep:
                    prt[c, i, q] = left[c][i]
                else:
                    store(it, q, pl.ds(0, 16), c, i, left[c][i], st[it, c, i, q + 2, 8:24, :])
        if not keep:
            add_square(it, left[0] + left[1])

    def finish(it, kind, t):
        rows = pl.ds(8 * t, 8)
        body_rows = pl.ds(8 + 8 * t, 8)
        face = faces[kind]

        def rim(at):
            real = [hal[it, kind, 0, j, at, rows, :] for j in range(6)]
            imag = [hal[it, kind, 1, j, at, rows, :] for j in range(6)]
            if kind == SAME:
                return [real, imag]
            return [
                [turn_cos * x - turn_sin * w for x, w in zip(real, imag)],
                [turn_sin * x + turn_cos * w for x, w in zip(real, imag)],
            ]

        near, far = rim(1 - face), rim(face)
        edge, second = 7 * face, 1 + 5 * face
        left = [[prt[c, i, edge, rows, :] for i in range(6)] for c in range(2)]
        for j in range(6):
            times(left, lambda i: nb[face, i, j, edge, rows, :], [near[c][j] for c in range(2)])
        squares = []
        for c in range(2):
            for i in range(6):
                residual = left[c][i] - ds[0, edge, rows, :] * far[c][i]
                squares.append(residual)
                store(it, edge, rows, c, i, residual, st[it, c, i, edge + 2, body_rows, :])
                residual = prt[c, i, second, rows, :] - ds[0, second, rows, :] * near[c][i]
                squares.append(residual)
                store(it, second, rows, c, i, residual, st[it, c, i, second + 2, body_rows, :])
        add_square(it, squares)

    every = (8, lambda i: i)
    inner = (4, lambda i: i + 2)
    outer = (4, lambda i: i + 4 * (i // 2))
    kinds = (OTHER, SAME)
    order = tuple((t, kind) for t in range(2) for kind in kinds)

    pitch_copy(0, kinds[0], 0).start()
    pitch_copy(0, kinds[1], 0).start()
    for way in range(2):
        span_start(0, way, 0)
    pitch_copy(0, kinds[0], 1).start()
    pitch_copy(0, kinds[1], 1).start()
    for d in range(1, 8):
        pl.semaphore_signal(ready_row, inc=1, device_id=row_peer(d), device_id_type=MESH)
    loads[0].wait()
    over(*every, lambda q: pack(0, q))
    axial_start(0, 0)
    for load in loads[1:]:
        load.wait()
    over(*every, lambda q: own_terms(0, q))
    pl.semaphore_wait(ready_row, 7)
    for d in range(1, 4):
        pl.semaphore_signal(ready, inc=1, device_id=plane_peer(d), device_id_type=MESH)
    side_wait(0, 0)
    over(*outer, lambda q: side_terms(0, q, True))
    for t in range(2):
        for kind in kinds:
            pitch_copy(0, kind, t).wait_recv()
            finish(0, kind, t)
            pitch_copy(1, kind, t).start()
            span_start(1, t, kind)
        if t == 0:
            over(*inner, lambda q: side_terms(0, q, False))
            for way in range(2):
                span_start(1, way, INNER)
            over(*inner, lambda q: pack(1, q))
            axial_start(1, INNER)
    over(*outer, lambda q: pack(1, q))
    for kind in range(2):
        axial_start(1, kind)

    over(*every, lambda q: own_terms(1, q))
    side_wait(1, INNER)
    over(*inner, lambda q: side_terms(1, q, False))
    for kind in range(2):
        side_wait(1, kind)
    over(*outer, lambda q: side_terms(1, q, True))
    for t, kind in order:
        pitch_copy(1, kind, t).wait_recv()
        finish(1, kind, t)

    half = lax.broadcasted_iota(jnp.int32, (1, 128), 1) < 64

    def folded(it):
        row = jnp.sum(sq[it], axis=0, keepdims=True)
        return row + pltpu.roll(row, 64, 1)

    total = jnp.where(half, folded(0), folded(1))
    me = (y * size_s + s) * 8 + x_hi * size_a + a
    tot_s[0:1] = total
    near = (0, 1, 2, 1)
    steps = sorted(
        ((dy, dz, dk) for dy in range(4) for dz in range(4) for dk in range(8) if dy + dz + dk > 0),
        key=lambda d: -(near[d[0]] + near[d[1]] + min(d[2], 8 - d[2]) / 2),
    )
    ys = [2 * lax.rem(y + d, size_p // 2) for d in range(4)]
    zs = [lax.rem(s + d, size_s) for d in range(4)]
    ks = [lax.rem(x_hi * size_a + a + d, 8) for d in range(8)]
    ks = [(k // size_a, lax.rem(k, size_a)) for k in ks]
    pl.semaphore_wait(ready, 3)
    for dy, dz, dk in steps:
        pltpu.make_async_remote_copy(
            src_ref=tot_s.at[pl.ds(0, 1)],
            dst_ref=red.at[pl.ds(me, 1)],
            send_sem=rsend.at[0],
            recv_sem=rrecv.at[0],
            device_id=(ys[dy] + ks[dk][0], zs[dz], ks[dk][1]),
            device_id_type=MESH,
        ).start()
    got = red.at[pl.ds(0, 127)]
    pltpu.make_async_copy(got, got, rrecv.at[0]).wait()
    index = lax.broadcasted_iota(jnp.int32, (128, 128), 0)
    total = total + jnp.sum(jnp.where(index == me, 0.0, red[...]), axis=0, keepdims=True)
    first_sum = jnp.sum(jnp.where(half, total, 0.0), axis=1, keepdims=True)
    second_sum = jnp.sum(jnp.where(half, 0.0, total), axis=1, keepdims=True)
    cells = float(12 * 8 * 16 * 128) * (size_p * size_s * size_a)
    lane1 = lax.broadcasted_iota(jnp.int32, (1, 128), 1)
    norms[...] = jnp.sqrt(jnp.where(lane1 == 0, first_sum, second_sum) / cells)

    for it in range(2):
        for t in range(2):
            for kind in range(2):
                pitch_copy(it, kind, t).wait_send()
        for group in range(1 if it == 0 else 3):
            side_drain(it, group)
    pltpu.make_async_copy(got, got, rsend.at[0]).wait()


def body(guess, right_side, diag_block, neighbour_blocks, dissipation, omega_volume, pseudo_step, phase):
    anywhere = pl.BlockSpec(memory_space=pltpu.HBM)
    dma = pltpu.SemaphoreType.DMA
    field, norms = pl.pallas_call(
        kernel,
        out_shape=(
            jax.ShapeDtypeStruct(guess.shape, F32),
            jax.ShapeDtypeStruct((1, 128), F32),
        ),
        in_specs=[anywhere] * 8,
        out_specs=(pl.BlockSpec(memory_space=pltpu.VMEM), pl.BlockSpec(memory_space=pltpu.VMEM)),
        scratch_shapes=[
            pltpu.VMEM((2, 2, 6, 12, 32, 128), F32),
            pltpu.VMEM((2, 2, 2, 6, 2, 16, 128), F32),
            pltpu.VMEM((2, 6, 8, 16, 128), F32),
            pltpu.VMEM((2, 6, 8, 16, 128), F32),
            pltpu.VMEM((6, 6, 8, 16, 128), jnp.bfloat16),
            pltpu.VMEM((6, 6, 6, 8, 16, 128), jnp.bfloat16),
            pltpu.VMEM((3, 8, 16, 128), F32),
            pltpu.VMEM((8, 16, 128), F32),
            pltpu.VMEM((8, 16, 128), F32),
            pltpu.VMEM((2, 8, 8, 128), F32),
            pltpu.VMEM((2, 2, 8, 8, 128), F32),
            pltpu.VMEM((2, 8, 128), F32),
            pltpu.VMEM((128, 128), F32),
            pltpu.VMEM((16, 128), F32),
            pltpu.SMEM((1,), F32),
            dma((14,)),
            dma((2, 2, 2)),
            dma((2, 2, 2)),
            dma((2, 2, 3)),
            dma((2, 2, 3)),
            dma((2, 2, 3)),
            dma((2, 2, 3)),
            dma((2,)),
            dma((2,)),
            pltpu.SemaphoreType.REGULAR,
            pltpu.SemaphoreType.REGULAR,
        ],
        compiler_params=pltpu.CompilerParams(
            collective_id=0, has_side_effects=True, vmem_limit_bytes=40 * 1024 * 1024
        ),
        name="tangent",
    )(*(
        pltpu.with_memory_space_constraint(operand, pltpu.HBM)
        for operand in (
            guess, right_side, diag_block, neighbour_blocks, dissipation, omega_volume, pseudo_step
        )
    ), phase)
    return field, norms[0, :2]


def solution(mesh):
    placed = (
        P(None, None, "pitch", "span", "axial"),
        P(None, None, "pitch", "span", "axial"),
        P(None, None, "pitch", "span", "axial"),
        P(None, None, None, "pitch", "span", "axial"),
        P(None, "pitch", "span", "axial"),
        P("pitch", "span", "axial"),
        P("pitch", "span", "axial"),
        P(),
    )
    return jax.shard_map(
        body,
        mesh=mesh,
        in_specs=placed,
        out_specs=(P(None, None, "pitch", "span", "axial"), P()),
        check_vma=False,
    )
```

```python
import functools

import jax
import jax.numpy as jnp
from jax import lax
from jax.experimental import pallas as pl
from jax.experimental.pallas import tpu as pltpu
from jax.sharding import PartitionSpec as P

ITERS = 2
MESH = pl.DeviceIdType.MESH
F32 = jnp.float32


def kernel(
    guess, right_h, diag_h, neigh_h, diss_h, omega_h, pseudo_h, phase_h,
    out, norms,
    st, hal, prt, rs, dg, nb, ds, om, ps, axs, axr, sq, red, tot_s, phase,
    ld_sem, psend, precv, zsend, zrecv, asend, arecv, rsend, rrecv, ready, ready_row,
):
    p, s, a = lax.axis_index("pitch"), lax.axis_index("span"), lax.axis_index("axial")
    size_p, size_s, size_a = lax.axis_size("pitch"), lax.axis_size("span"), lax.axis_size("axial")
    y, x_hi = p // 2, lax.rem(p, 2)

    def row_peer(d):
        k = lax.rem(x_hi * size_a + a + d, 2 * size_a)
        return (y * 2 + k // size_a, s, lax.rem(k, size_a))

    def plane_peer(d):
        dy, dz = d // 4, d % 4
        return (lax.rem(p + 2 * dy, size_p), lax.rem(s + dz, size_s), a)

    other = lax.rem(p - 1 + 2 * x_hi + size_p, size_p)
    bar = pltpu.get_barrier_semaphore()
    peers = [(other, s, a)]
    peers += [row_peer(d) for d in range(1, 8)]
    peers += [plane_peer(4 * d) for d in range(1, 4)]
    peers += [plane_peer(d) for d in range(1, 4)]
    for peer in peers:
        pl.semaphore_signal(bar, inc=1, device_id=peer, device_id_type=MESH)

    loads = [
        pltpu.make_async_copy(guess, st.at[0, :, :, pl.ds(2, 8), pl.ds(8, 16), :], ld_sem.at[0]),
        pltpu.make_async_copy(diss_h, ds, ld_sem.at[1]),
        pltpu.make_async_copy(omega_h, om, ld_sem.at[2]),
        pltpu.make_async_copy(pseudo_h, ps, ld_sem.at[3]),
        pltpu.make_async_copy(right_h, rs, ld_sem.at[4]),
        pltpu.make_async_copy(diag_h, dg, ld_sem.at[5]),
    ] + [pltpu.make_async_copy(neigh_h.at[d], nb.at[d], ld_sem.at[6 + d]) for d in range(6)]
    lane = lax.broadcasted_iota(jnp.int32, (8, 128), 1)
    faces = (x_hi, 1 - x_hi)
    OTHER, SAME = 0, 1

    pl.semaphore_wait(bar, len(peers))

    def pitch_copy(it, kind, t):
        face = faces[kind]
        layers = pl.ds(6 * face, 2)
        if it == 0:
            src = guess.at[:, :, layers, pl.ds(8 * t, 8), :]
        else:
            src = st.at[1, :, :, pl.ds(2 + 6 * face, 2), pl.ds(8 + 8 * t, 8), :]
        return pltpu.make_async_remote_copy(
            src_ref=src,
            dst_ref=hal.at[it, kind, :, :, :, pl.ds(8 * t, 8), :],
            send_sem=psend.at[it, kind, t],
            recv_sem=precv.at[it, kind, t],
            device_id=(lax.rem(p + size_p - 1 + 2 * face, size_p), s, a),
            device_id_type=MESH,
        )

    INNER = 2
    groups = ((6 * faces[0], 2), (6 * faces[1], 2), (2, 4))

    def span_copy(it, way, group):
        first_layer, count = (0, 8) if it == 0 else groups[group]
        row = 0 if way == 0 else 14
        if it == 0:
            src = guess.at[:, :, pl.ds(first_layer, count), pl.ds(row, 2), :]
        else:
            src = st.at[1, :, :, pl.ds(2 + first_layer, count), pl.ds(8 + row, 2), :]
        return pltpu.make_async_remote_copy(
            src_ref=src,
            dst_ref=st.at[it, :, :, pl.ds(2 + first_layer, count), pl.ds(24 if way == 0 else 6, 2), :],
            send_sem=zsend.at[it, way, group],
            recv_sem=zrecv.at[it, 1 - way, group],
            device_id=(p, lax.rem(s + (size_s - 1 if way == 0 else 1), size_s), a),
            device_id_type=MESH,
        )

    def axial_copy(it, way, group):
        first_layer, count = (0, 8) if it == 0 else groups[group]
        return pltpu.make_async_remote_copy(
            src_ref=axs.at[it, pl.ds(first_layer, count)],
            dst_ref=axr.at[it, 1 - way, pl.ds(first_layer, count)],
            send_sem=asend.at[it, way, group],
            recv_sem=arecv.at[it, 1 - way, group],
            device_id=(p, s, lax.rem(a + (size_a - 1 if way == 0 else 1), size_a)),
            device_id_type=MESH,
        )

    has_span = (s > 0, s < size_s - 1)
    has_axial = (a > 0, a < size_a - 1)

    def span_start(it, way, group):
        @pl.when(has_span[way])
        def _():
            span_copy(it, way, group).start()

    def axial_start(it, group):
        for way in range(2):
            @pl.when(has_axial[way])
            def _():
                axial_copy(it, way, group).start()

    def side_wait(it, group):
        for way in range(2):
            @pl.when(has_span[way])
            def _():
                span_copy(it, 1 - way, group).wait_recv()

            @pl.when(has_axial[way])
            def _():
                axial_copy(it, 1 - way, group).wait_recv()

    def side_drain(it, group):
        for way in range(2):
            @pl.when(has_span[way])
            def _():
                span_copy(it, way, group).wait_send()

            @pl.when(has_axial[way])
            def _():
                axial_copy(it, way, group).wait_send()

    def over(count, layer_of, work):
        def step(i, carry):
            work(layer_of(i))
            return carry

        lax.fori_loop(0, count, step, 0)

    def pack(it, q):
        packed = jnp.zeros((8, 128), F32)
        for c in range(2):
            for v in range(6):
                for t in range(2):
                    k = (c * 6 + v) * 2 + t
                    tile = st[it, c, v, q + 2, 8 + 8 * t : 16 + 8 * t, :]
                    packed = jnp.where(lane // 4 == k, pltpu.roll(tile, 4 * k + 2, 1), packed)
        axs[it, q] = packed

    def store(it, q, rows, c, v, residual, state):
        new = state + ps[q, rows, :] * residual
        if it == ITERS - 1:
            out[c, v, q, rows, :] = new
        else:
            st[1, c, v, q + 2, pl.ds(8 + rows.start, rows.size), :] = new

    def add_square(it, residuals):
        total = sq[it]
        for residual in residuals:
            square = residual * residual
            for t in range(residual.shape[0] // 8):
                total = total + square[8 * t : 8 * t + 8]
        sq[it] = total

    def times(left, block_of, values):
        for i in range(6):
            block = block_of(i).astype(F32)
            for c in range(2):
                left[c][i] = left[c][i] - block * values[c]

    def own_terms(it, q):
        left = [[rs[c, i, q] for i in range(6)] for c in range(2)]
        for j in range(6):
            times(left, lambda i: dg[i, j, q], [st[it, c, j, q + 2, 8:24, :] for c in range(2)])
        for d in range(2):
            for j in range(6):
                times(left, lambda i: nb[d, i, j, q], [st[it, c, j, q + 1 + 2 * d, 8:24, :] for c in range(2)])
        for i in range(6):
            for c in range(2):
                value = left[c][i]
                value = value - ds[0, q] * (st[it, c, i, q, 8:24, :] + st[it, c, i, q + 4, 8:24, :])
                turned = om[q] * st[it, 1 - c, i, q + 2, 8:24, :]
                prt[c, i, q] = value + turned if c == 0 else value - turned

    def side_terms(it, q, t, keep):
        lo = 8 + 8 * t
        rows = pl.ds(8 * t, 8)
        left = [[prt[c, i, q, rows, :] for i in range(6)] for c in range(2)]
        for d in range(2):
            for j in range(6):
                at = lo - 1 + 2 * d
                times(left, lambda i: nb[2 + d, i, j, q, rows, :], [st[it, c, j, q + 2, at : at + 8, :] for c in range(2)])
        mixed = jnp.where(lax.rem(lane, 4) < 2, axr[it, 0, q], axr[it, 1, q])
        for j in range(6):
            below, above = [], []
            for c in range(2):
                u = st[it, c, j, q + 2, lo : lo + 8, :]
                k = (c * 6 + j) * 2 + t
                rim = pltpu.roll(mixed, 126 - 4 * k, 1)
                below.append(pltpu.roll(jnp.where(lane == 127, rim, u), 1, 1))
                above.append(pltpu.roll(jnp.where(lane == 0, rim, u), 127, 1))
                left[c][j] = left[c][j] - ds[2, q, rows, :] * (
                    pltpu.roll(jnp.where(lane >= 126, rim, u), 2, 1)
                    + pltpu.roll(jnp.where(lane < 2, rim, u), 126, 1)
                )
            times(left, lambda i: nb[4, i, j, q, rows, :], below)
            times(left, lambda i: nb[5, i, j, q, rows, :], above)
        for i in range(6):
            for c in range(2):
                left[c][i] = left[c][i] - ds[1, q, rows, :] * (
                    st[it, c, i, q + 2, lo - 2 : lo + 6, :] + st[it, c, i, q + 2, lo + 2 : lo + 10, :]
                )
                if keep:
                    prt[c, i, q, rows, :] = left[c][i]
                else:
                    store(it, q, rows, c, i, left[c][i], st[it, c, i, q + 2, lo : lo + 8, :])
        if not keep:
            add_square(it, left[0] + left[1])

    def finish(it, kind, t):
        rows = pl.ds(8 * t, 8)
        body_rows = pl.ds(8 + 8 * t, 8)
        face = faces[kind]

        def rim(at):
            real = [hal[it, kind, 0, j, at, rows, :] for j in range(6)]
            imag = [hal[it, kind, 1, j, at, rows, :] for j in range(6)]
            if kind == SAME:
                return [real, imag]
            return [
                [turn_cos * x - turn_sin * w for x, w in zip(real, imag)],
                [turn_sin * x + turn_cos * w for x, w in zip(real, imag)],
            ]

        near, far = rim(1 - face), rim(face)
        edge, second = 7 * face, 1 + 5 * face
        left = [[prt[c, i, edge, rows, :] for i in range(6)] for c in range(2)]
        for j in range(6):
            times(left, lambda i: nb[face, i, j, edge, rows, :], [near[c][j] for c in range(2)])
        squares = []
        for c in range(2):
            for i in range(6):
                residual = left[c][i] - ds[0, edge, rows, :] * far[c][i]
                squares.append(residual)
                store(it, edge, rows, c, i, residual, st[it, c, i, edge + 2, body_rows, :])
                residual = prt[c, i, second, rows, :] - ds[0, second, rows, :] * near[c][i]
                squares.append(residual)
                store(it, second, rows, c, i, residual, st[it, c, i, second + 2, body_rows, :])
        add_square(it, squares)

    every = (8, lambda i: i)
    inner = (4, lambda i: i + 2)
    outer = (4, lambda i: i + 4 * (i // 2))
    kinds = (OTHER, SAME)
    order = tuple((t, kind) for t in range(2) for kind in kinds)

    pitch_copy(0, kinds[0], 0).start()
    pitch_copy(0, kinds[1], 0).start()
    for way in range(2):
        span_start(0, way, 0)
    pitch_copy(0, kinds[0], 1).start()
    pitch_copy(0, kinds[1], 1).start()
    phase_load = pltpu.make_async_copy(phase_h, phase, ld_sem.at[12])
    phase_load.start()
    for load in loads:
        load.start()

    for d in range(1, 8):
        pl.semaphore_signal(ready_row, inc=1, device_id=row_peer(d), device_id_type=MESH)
    rows_zero = jnp.zeros((2, 2, 6, 8, 2, 128), F32)
    ax_zero = jnp.zeros((2, 8, 8, 128), F32)
    layers_zero = jnp.zeros((2, 2, 6, 2, 16, 128), F32)
    st[:, :, :, 0:2, 8:24, :] = layers_zero
    st[:, :, :, 10:12, 8:24, :] = layers_zero

    @pl.when(s == 0)
    def _():
        st[:, :, :, 2:10, 6:8, :] = rows_zero

    @pl.when(s == size_s - 1)
    def _():
        st[:, :, :, 2:10, 24:26, :] = rows_zero

    @pl.when(a == 0)
    def _():
        axr[:, 0] = ax_zero

    @pl.when(a == size_a - 1)
    def _():
        axr[:, 1] = ax_zero

    sq[...] = jnp.zeros((2, 8, 128), F32)
    loads[0].wait()
    over(*every, lambda q: pack(0, q))
    axial_start(0, 0)
    for load in loads[1:]:
        load.wait()
    over(*every, lambda q: own_terms(0, q))
    pl.semaphore_wait(ready_row, 7)
    for d in range(1, 4):
        pl.semaphore_signal(ready, inc=1, device_id=plane_peer(d), device_id_type=MESH)
    phase_load.wait()
    angle = jnp.full((8, 128), phase[0], F32)
    cosine, sine = jnp.cos(angle), jnp.sin(angle)
    first, last = p == 0, p == size_p - 1
    turn_cos = jnp.where(first | last, cosine, 1.0)
    turn_sin = jnp.where(first, -sine, jnp.where(last, sine, 0.0))
    side_wait(0, 0)
    for t in range(2):
        over(*outer, lambda q: side_terms(0, q, t, True))
        for kind in kinds:
            pitch_copy(0, kind, t).wait_recv()
            finish(0, kind, t)
            span_start(1, t, kind)
            if t == 1:
                over(2, lambda i: i + 6 * faces[kind], lambda q: pack(1, q))
                axial_start(1, kind)
            pitch_copy(1, kind, t).start()
        if t == 0:
            for half_rows in range(2):
                over(*inner, lambda q: side_terms(0, q, half_rows, False))
            for way in range(2):
                span_start(1, way, INNER)
            over(*inner, lambda q: pack(1, q))
            axial_start(1, INNER)

    over(*every, lambda q: own_terms(1, q))
    side_wait(1, INNER)
    for t in range(2):
        over(*inner, lambda q: side_terms(1, q, t, False))
    for kind in range(2):
        side_wait(1, kind)
    for t in range(2):
        over(*outer, lambda q: side_terms(1, q, t, True))
    for t, kind in order:
        pitch_copy(1, kind, t).wait_recv()
        finish(1, kind, t)

    half = lax.broadcasted_iota(jnp.int32, (1, 128), 1) < 64

    def folded(it):
        row = jnp.sum(sq[it], axis=0, keepdims=True)
        return row + pltpu.roll(row, 64, 1)

    total = jnp.where(half, folded(0), folded(1))
    me = (y * size_s + s) * 8 + x_hi * size_a + a
    tot_s[0:1] = total
    near = (0, 1, 2, 1)
    steps = sorted(
        ((dy, dz, dk) for dy in range(4) for dz in range(4) for dk in range(8) if dy + dz + dk > 0),
        key=lambda d: -(near[d[0]] + near[d[1]] + min(d[2], 8 - d[2]) / 2),
    )
    ys = [2 * lax.rem(y + d, size_p // 2) for d in range(4)]
    zs = [lax.rem(s + d, size_s) for d in range(4)]
    ks = [lax.rem(x_hi * size_a + a + d, 8) for d in range(8)]
    ks = [(k // size_a, lax.rem(k, size_a)) for k in ks]
    pl.semaphore_wait(ready, 3)
    for dy, dz, dk in steps:
        pltpu.make_async_remote_copy(
            src_ref=tot_s.at[pl.ds(0, 1)],
            dst_ref=red.at[pl.ds(me, 1)],
            send_sem=rsend.at[0],
            recv_sem=rrecv.at[0],
            device_id=(ys[dy] + ks[dk][0], zs[dz], ks[dk][1]),
            device_id_type=MESH,
        ).start()
    got = red.at[pl.ds(0, 127)]
    pltpu.make_async_copy(got, got, rrecv.at[0]).wait()
    index = lax.broadcasted_iota(jnp.int32, (128, 128), 0)
    total = total + jnp.sum(jnp.where(index == me, 0.0, red[...]), axis=0, keepdims=True)
    first_sum = jnp.sum(jnp.where(half, total, 0.0), axis=1, keepdims=True)
    second_sum = jnp.sum(jnp.where(half, 0.0, total), axis=1, keepdims=True)
    cells = float(12 * 8 * 16 * 128) * (size_p * size_s * size_a)
    lane1 = lax.broadcasted_iota(jnp.int32, (1, 128), 1)
    norms[...] = jnp.sqrt(jnp.where(lane1 == 0, first_sum, second_sum) / cells)

    for it in range(2):
        for t in range(2):
            for kind in range(2):
                pitch_copy(it, kind, t).wait_send()
        for group in range(1 if it == 0 else 3):
            side_drain(it, group)
    pltpu.make_async_copy(got, got, rsend.at[0]).wait()


def body(guess, right_side, diag_block, neighbour_blocks, dissipation, omega_volume, pseudo_step, phase):
    anywhere = pl.BlockSpec(memory_space=pltpu.HBM)
    dma = pltpu.SemaphoreType.DMA
    field, norms = pl.pallas_call(
        kernel,
        out_shape=(
            jax.ShapeDtypeStruct(guess.shape, F32),
            jax.ShapeDtypeStruct((1, 128), F32),
        ),
        in_specs=[anywhere] * 8,
        out_specs=(pl.BlockSpec(memory_space=pltpu.VMEM), pl.BlockSpec(memory_space=pltpu.VMEM)),
        scratch_shapes=[
            pltpu.VMEM((2, 2, 6, 12, 32, 128), F32),
            pltpu.VMEM((2, 2, 2, 6, 2, 16, 128), F32),
            pltpu.VMEM((2, 6, 8, 16, 128), F32),
            pltpu.VMEM((2, 6, 8, 16, 128), F32),
            pltpu.VMEM((6, 6, 8, 16, 128), jnp.bfloat16),
            pltpu.VMEM((6, 6, 6, 8, 16, 128), jnp.bfloat16),
            pltpu.VMEM((3, 8, 16, 128), F32),
            pltpu.VMEM((8, 16, 128), F32),
            pltpu.VMEM((8, 16, 128), F32),
            pltpu.VMEM((2, 8, 8, 128), F32),
            pltpu.VMEM((2, 2, 8, 8, 128), F32),
            pltpu.VMEM((2, 8, 128), F32),
            pltpu.VMEM((128, 128), F32),
            pltpu.VMEM((16, 128), F32),
            pltpu.SMEM((1,), F32),
            dma((14,)),
            dma((2, 2, 2)),
            dma((2, 2, 2)),
            dma((2, 2, 3)),
            dma((2, 2, 3)),
            dma((2, 2, 3)),
            dma((2, 2, 3)),
            dma((2,)),
            dma((2,)),
            pltpu.SemaphoreType.REGULAR,
            pltpu.SemaphoreType.REGULAR,
        ],
        compiler_params=pltpu.CompilerParams(
            collective_id=0, has_side_effects=True, vmem_limit_bytes=40 * 1024 * 1024
        ),
        name="tangent",
    )(*(
        pltpu.with_memory_space_constraint(operand, pltpu.HBM)
        for operand in (
            guess, right_side, diag_block, neighbour_blocks, dissipation, omega_volume, pseudo_step
        )
    ), phase)
    return field, norms[0, :2]


def solution(mesh):
    placed = (
        P(None, None, "pitch", "span", "axial"),
        P(None, None, "pitch", "span", "axial"),
        P(None, None, "pitch", "span", "axial"),
        P(None, None, None, "pitch", "span", "axial"),
        P(None, "pitch", "span", "axial"),
        P("pitch", "span", "axial"),
        P("pitch", "span", "axial"),
        P(),
    )
    return jax.shard_map(
        body,
        mesh=mesh,
        in_specs=placed,
        out_specs=(P(None, None, "pitch", "span", "axial"), P()),
        check_vma=False,
    )
```

```python
import functools

import jax
import jax.numpy as jnp
from jax import lax
from jax.experimental import pallas as pl
from jax.experimental.pallas import tpu as pltpu
from jax.sharding import PartitionSpec as P

ITERS = 2
MESH = pl.DeviceIdType.MESH
F32 = jnp.float32


def kernel(
    guess, right_h, diag_h, neigh_h, diss_h, omega_h, pseudo_h, phase_h,
    out, norms,
    st, hal, prt, rs, dg, nb, ds, om, ps, axs, axr, sq, red, tot_s, phase,
    ld_sem, psend, precv, zsend, zrecv, asend, arecv, rsend, rrecv, ready, ready_row,
):
    p, s, a = lax.axis_index("pitch"), lax.axis_index("span"), lax.axis_index("axial")
    size_p, size_s, size_a = lax.axis_size("pitch"), lax.axis_size("span"), lax.axis_size("axial")
    y, x_hi = p // 2, lax.rem(p, 2)

    def row_peer(d):
        k = lax.rem(x_hi * size_a + a + d, 2 * size_a)
        return (y * 2 + k // size_a, s, lax.rem(k, size_a))

    def plane_peer(d):
        dy, dz = d // 4, d % 4
        return (lax.rem(p + 2 * dy, size_p), lax.rem(s + dz, size_s), a)

    other = lax.rem(p - 1 + 2 * x_hi + size_p, size_p)
    bar = pltpu.get_barrier_semaphore()
    peers = [(other, s, a)]
    peers += [row_peer(d) for d in range(1, 8)]
    peers += [plane_peer(4 * d) for d in range(1, 4)]
    peers += [plane_peer(d) for d in range(1, 4)]
    for peer in peers:
        pl.semaphore_signal(bar, inc=1, device_id=peer, device_id_type=MESH)

    loads = [
        pltpu.make_async_copy(guess, st.at[0, :, :, pl.ds(2, 8), pl.ds(8, 16), :], ld_sem.at[0]),
        pltpu.make_async_copy(diss_h, ds, ld_sem.at[1]),
        pltpu.make_async_copy(omega_h, om, ld_sem.at[2]),
        pltpu.make_async_copy(pseudo_h, ps, ld_sem.at[3]),
        pltpu.make_async_copy(right_h, rs, ld_sem.at[4]),
        pltpu.make_async_copy(diag_h, dg, ld_sem.at[5]),
    ] + [pltpu.make_async_copy(neigh_h.at[d], nb.at[d], ld_sem.at[6 + d]) for d in range(6)]
    lane = lax.broadcasted_iota(jnp.int32, (8, 128), 1)
    faces = (x_hi, 1 - x_hi)
    OTHER, SAME = 0, 1

    pl.semaphore_wait(bar, len(peers))

    def pitch_copy(it, kind, t):
        face = faces[kind]
        layers = pl.ds(6 * face, 2)
        if it == 0:
            src = guess.at[:, :, layers, pl.ds(8 * t, 8), :]
        else:
            src = st.at[1, :, :, pl.ds(2 + 6 * face, 2), pl.ds(8 + 8 * t, 8), :]
        return pltpu.make_async_remote_copy(
            src_ref=src,
            dst_ref=hal.at[it, kind, :, :, :, pl.ds(8 * t, 8), :],
            send_sem=psend.at[it, kind, t],
            recv_sem=precv.at[it, kind, t],
            device_id=(lax.rem(p + size_p - 1 + 2 * face, size_p), s, a),
            device_id_type=MESH,
        )

    INNER = 2
    groups = ((6 * faces[0], 2), (6 * faces[1], 2), (2, 4))

    def span_copy(it, way, group):
        first_layer, count = (0, 8) if it == 0 else groups[group]
        row = 0 if way == 0 else 14
        if it == 0:
            src = guess.at[:, :, pl.ds(first_layer, count), pl.ds(row, 2), :]
        else:
            src = st.at[1, :, :, pl.ds(2 + first_layer, count), pl.ds(8 + row, 2), :]
        return pltpu.make_async_remote_copy(
            src_ref=src,
            dst_ref=st.at[it, :, :, pl.ds(2 + first_layer, count), pl.ds(24 if way == 0 else 6, 2), :],
            send_sem=zsend.at[it, way, group],
            recv_sem=zrecv.at[it, 1 - way, group],
            device_id=(p, lax.rem(s + (size_s - 1 if way == 0 else 1), size_s), a),
            device_id_type=MESH,
        )

    def axial_copy(it, way, group):
        first_layer, count = (0, 8) if it == 0 else groups[group]
        return pltpu.make_async_remote_copy(
            src_ref=axs.at[it, pl.ds(first_layer, count)],
            dst_ref=axr.at[it, 1 - way, pl.ds(first_layer, count)],
            send_sem=asend.at[it, way, group],
            recv_sem=arecv.at[it, 1 - way, group],
            device_id=(p, s, lax.rem(a + (size_a - 1 if way == 0 else 1), size_a)),
            device_id_type=MESH,
        )

    has_span = (s > 0, s < size_s - 1)
    has_axial = (a > 0, a < size_a - 1)

    def span_start(it, way, group):
        @pl.when(has_span[way])
        def _():
            span_copy(it, way, group).start()

    def axial_start(it, group):
        for way in range(2):
            @pl.when(has_axial[way])
            def _():
                axial_copy(it, way, group).start()

    def side_wait(it, group):
        for way in range(2):
            @pl.when(has_span[way])
            def _():
                span_copy(it, 1 - way, group).wait_recv()

            @pl.when(has_axial[way])
            def _():
                axial_copy(it, 1 - way, group).wait_recv()

    def side_drain(it, group):
        for way in range(2):
            @pl.when(has_span[way])
            def _():
                span_copy(it, way, group).wait_send()

            @pl.when(has_axial[way])
            def _():
                axial_copy(it, way, group).wait_send()

    def over(count, layer_of, work):
        def step(i, carry):
            work(layer_of(i))
            return carry

        lax.fori_loop(0, count, step, 0)

    def pack(it, q, halves=(0, 1)):
        packed = jnp.zeros((8, 128), F32) if halves[0] == 0 else axs[it, q]
        for c in range(2):
            for v in range(6):
                for t in halves:
                    k = (c * 6 + v) * 2 + t
                    tile = st[it, c, v, q + 2, 8 + 8 * t : 16 + 8 * t, :]
                    packed = jnp.where(lane // 4 == k, pltpu.roll(tile, 4 * k + 2, 1), packed)
        axs[it, q] = packed

    def store(it, q, rows, c, v, residual, state):
        new = state + ps[q, rows, :] * residual
        if it == ITERS - 1:
            out[c, v, q, rows, :] = new
        else:
            st[1, c, v, q + 2, pl.ds(8 + rows.start, rows.size), :] = new

    def add_square(it, residuals):
        total = sq[it]
        for residual in residuals:
            square = residual * residual
            for t in range(residual.shape[0] // 8):
                total = total + square[8 * t : 8 * t + 8]
        sq[it] = total

    def times(left, block_of, values):
        for i in range(6):
            block = block_of(i).astype(F32)
            for c in range(2):
                left[c][i] = left[c][i] - block * values[c]

    def own_terms(it, q):
        left = [[rs[c, i, q] for i in range(6)] for c in range(2)]
        for j in range(6):
            times(left, lambda i: dg[i, j, q], [st[it, c, j, q + 2, 8:24, :] for c in range(2)])
        for d in range(2):
            for j in range(6):
                times(left, lambda i: nb[d, i, j, q], [st[it, c, j, q + 1 + 2 * d, 8:24, :] for c in range(2)])
        for i in range(6):
            for c in range(2):
                value = left[c][i]
                value = value - ds[0, q] * (st[it, c, i, q, 8:24, :] + st[it, c, i, q + 4, 8:24, :])
                turned = om[q] * st[it, 1 - c, i, q + 2, 8:24, :]
                prt[c, i, q] = value + turned if c == 0 else value - turned

    def side_terms(it, q, t, keep):
        lo = 8 + 8 * t
        rows = pl.ds(8 * t, 8)
        left = [[prt[c, i, q, rows, :] for i in range(6)] for c in range(2)]
        for d in range(2):
            for j in range(6):
                at = lo - 1 + 2 * d
                times(left, lambda i: nb[2 + d, i, j, q, rows, :], [st[it, c, j, q + 2, at : at + 8, :] for c in range(2)])
        mixed = jnp.where(lax.rem(lane, 4) < 2, axr[it, 0, q], axr[it, 1, q])
        for j in range(6):
            below, above = [], []
            for c in range(2):
                u = st[it, c, j, q + 2, lo : lo + 8, :]
                k = (c * 6 + j) * 2 + t
                rim = pltpu.roll(mixed, 126 - 4 * k, 1)
                below.append(pltpu.roll(jnp.where(lane == 127, rim, u), 1, 1))
                above.append(pltpu.roll(jnp.where(lane == 0, rim, u), 127, 1))
                left[c][j] = left[c][j] - ds[2, q, rows, :] * (
                    pltpu.roll(jnp.where(lane >= 126, rim, u), 2, 1)
                    + pltpu.roll(jnp.where(lane < 2, rim, u), 126, 1)
                )
            times(left, lambda i: nb[4, i, j, q, rows, :], below)
            times(left, lambda i: nb[5, i, j, q, rows, :], above)
        for i in range(6):
            for c in range(2):
                left[c][i] = left[c][i] - ds[1, q, rows, :] * (
                    st[it, c, i, q + 2, lo - 2 : lo + 6, :] + st[it, c, i, q + 2, lo + 2 : lo + 10, :]
                )
                if keep:
                    prt[c, i, q, rows, :] = left[c][i]
                else:
                    store(it, q, rows, c, i, left[c][i], st[it, c, i, q + 2, lo : lo + 8, :])
        if not keep:
            add_square(it, left[0] + left[1])

    def finish(it, kind, t):
        rows = pl.ds(8 * t, 8)
        body_rows = pl.ds(8 + 8 * t, 8)
        face = faces[kind]

        def rim(at):
            real = [hal[it, kind, 0, j, at, rows, :] for j in range(6)]
            imag = [hal[it, kind, 1, j, at, rows, :] for j in range(6)]
            if kind == SAME:
                return [real, imag]
            return [
                [turn_cos * x - turn_sin * w for x, w in zip(real, imag)],
                [turn_sin * x + turn_cos * w for x, w in zip(real, imag)],
            ]

        near, far = rim(1 - face), rim(face)
        edge, second = 7 * face, 1 + 5 * face
        left = [[prt[c, i, edge, rows, :] for i in range(6)] for c in range(2)]
        for j in range(6):
            times(left, lambda i: nb[face, i, j, edge, rows, :], [near[c][j] for c in range(2)])
        squares = []
        for c in range(2):
            for i in range(6):
                residual = left[c][i] - ds[0, edge, rows, :] * far[c][i]
                squares.append(residual)
                store(it, edge, rows, c, i, residual, st[it, c, i, edge + 2, body_rows, :])
                residual = prt[c, i, second, rows, :] - ds[0, second, rows, :] * near[c][i]
                squares.append(residual)
                store(it, second, rows, c, i, residual, st[it, c, i, second + 2, body_rows, :])
        add_square(it, squares)

    every = (8, lambda i: i)
    inner = (4, lambda i: i + 2)
    outer = (4, lambda i: i + 4 * (i // 2))
    kinds = (OTHER, SAME)
    order = tuple((t, kind) for t in range(2) for kind in kinds)

    pitch_copy(0, kinds[0], 0).start()
    pitch_copy(0, kinds[1], 0).start()
    for way in range(2):
        span_start(0, way, 0)
    pitch_copy(0, kinds[0], 1).start()
    pitch_copy(0, kinds[1], 1).start()
    phase_load = pltpu.make_async_copy(phase_h, phase, ld_sem.at[12])
    phase_load.start()
    for load in loads:
        load.start()

    for d in range(1, 8):
        pl.semaphore_signal(ready_row, inc=1, device_id=row_peer(d), device_id_type=MESH)
    rows_zero = jnp.zeros((2, 2, 6, 8, 2, 128), F32)
    ax_zero = jnp.zeros((2, 8, 8, 128), F32)
    layers_zero = jnp.zeros((2, 2, 6, 2, 16, 128), F32)
    st[:, :, :, 0:2, 8:24, :] = layers_zero
    st[:, :, :, 10:12, 8:24, :] = layers_zero

    @pl.when(s == 0)
    def _():
        st[:, :, :, 2:10, 6:8, :] = rows_zero

    @pl.when(s == size_s - 1)
    def _():
        st[:, :, :, 2:10, 24:26, :] = rows_zero

    @pl.when(a == 0)
    def _():
        axr[:, 0] = ax_zero

    @pl.when(a == size_a - 1)
    def _():
        axr[:, 1] = ax_zero

    sq[...] = jnp.zeros((2, 8, 128), F32)
    loads[0].wait()
    over(*every, lambda q: pack(0, q))
    axial_start(0, 0)
    for load in loads[1:]:
        load.wait()
    over(*every, lambda q: own_terms(0, q))
    pl.semaphore_wait(ready_row, 7)
    for d in range(1, 4):
        pl.semaphore_signal(ready, inc=1, device_id=plane_peer(d), device_id_type=MESH)
    phase_load.wait()
    angle = jnp.full((8, 128), phase[0], F32)
    cosine, sine = jnp.cos(angle), jnp.sin(angle)
    first, last = p == 0, p == size_p - 1
    turn_cos = jnp.where(first | last, cosine, 1.0)
    turn_sin = jnp.where(first, -sine, jnp.where(last, sine, 0.0))
    side_wait(0, 0)
    for t in range(2):
        over(*outer, lambda q: side_terms(0, q, t, True))
        for kind in kinds:
            pitch_copy(0, kind, t).wait_recv()
            finish(0, kind, t)
            span_start(1, t, kind)
            if t == 1:
                over(2, lambda i: i + 6 * faces[kind], lambda q: pack(1, q, (1,)))
                axial_start(1, kind)
            pitch_copy(1, kind, t).start()
        if t == 0:
            over(*outer, lambda q: pack(1, q, (0,)))
            for half_rows in range(2):
                over(*inner, lambda q: side_terms(0, q, half_rows, False))
            for way in range(2):
                span_start(1, way, INNER)
            over(*inner, lambda q: pack(1, q))
            axial_start(1, INNER)

    over(*every, lambda q: own_terms(1, q))
    side_wait(1, INNER)
    for t in range(2):
        over(*inner, lambda q: side_terms(1, q, t, False))
    for kind in range(2):
        side_wait(1, kind)
    for t in range(2):
        over(*outer, lambda q: side_terms(1, q, t, True))
    for t, kind in order:
        pitch_copy(1, kind, t).wait_recv()
        finish(1, kind, t)

    half = lax.broadcasted_iota(jnp.int32, (1, 128), 1) < 64

    def folded(it):
        row = jnp.sum(sq[it], axis=0, keepdims=True)
        return row + pltpu.roll(row, 64, 1)

    total = jnp.where(half, folded(0), folded(1))
    me = (y * size_s + s) * 8 + x_hi * size_a + a
    tot_s[0:1] = total
    near = (0, 1, 2, 1)
    steps = sorted(
        ((dy, dz, dk) for dy in range(4) for dz in range(4) for dk in range(8) if dy + dz + dk > 0),
        key=lambda d: -(near[d[0]] + near[d[1]] + min(d[2], 8 - d[2]) / 2),
    )
    ys = [2 * lax.rem(y + d, size_p // 2) for d in range(4)]
    zs = [lax.rem(s + d, size_s) for d in range(4)]
    ks = [lax.rem(x_hi * size_a + a + d, 8) for d in range(8)]
    ks = [(k // size_a, lax.rem(k, size_a)) for k in ks]
    pl.semaphore_wait(ready, 3)
    for dy, dz, dk in steps:
        pltpu.make_async_remote_copy(
            src_ref=tot_s.at[pl.ds(0, 1)],
            dst_ref=red.at[pl.ds(me, 1)],
            send_sem=rsend.at[0],
            recv_sem=rrecv.at[0],
            device_id=(ys[dy] + ks[dk][0], zs[dz], ks[dk][1]),
            device_id_type=MESH,
        ).start()
    for it in range(2):
        for t in range(2):
            for kind in range(2):
                pitch_copy(it, kind, t).wait_send()
        for group in range(1 if it == 0 else 3):
            side_drain(it, group)
    got = red.at[pl.ds(0, 127)]
    pltpu.make_async_copy(got, got, rrecv.at[0]).wait()
    index = lax.broadcasted_iota(jnp.int32, (128, 128), 0)
    total = total + jnp.sum(jnp.where(index == me, 0.0, red[...]), axis=0, keepdims=True)
    first_sum = jnp.sum(jnp.where(half, total, 0.0), axis=1, keepdims=True)
    second_sum = jnp.sum(jnp.where(half, 0.0, total), axis=1, keepdims=True)
    cells = float(12 * 8 * 16 * 128) * (size_p * size_s * size_a)
    lane1 = lax.broadcasted_iota(jnp.int32, (1, 128), 1)
    norms[...] = jnp.sqrt(jnp.where(lane1 == 0, first_sum, second_sum) / cells)

    pltpu.make_async_copy(got, got, rsend.at[0]).wait()


def body(guess, right_side, diag_block, neighbour_blocks, dissipation, omega_volume, pseudo_step, phase):
    anywhere = pl.BlockSpec(memory_space=pltpu.HBM)
    dma = pltpu.SemaphoreType.DMA
    field, norms = pl.pallas_call(
        kernel,
        out_shape=(
            jax.ShapeDtypeStruct(guess.shape, F32),
            jax.ShapeDtypeStruct((1, 128), F32),
        ),
        in_specs=[anywhere] * 8,
        out_specs=(pl.BlockSpec(memory_space=pltpu.VMEM), pl.BlockSpec(memory_space=pltpu.VMEM)),
        scratch_shapes=[
            pltpu.VMEM((2, 2, 6, 12, 32, 128), F32),
            pltpu.VMEM((2, 2, 2, 6, 2, 16, 128), F32),
            pltpu.VMEM((2, 6, 8, 16, 128), F32),
            pltpu.VMEM((2, 6, 8, 16, 128), F32),
            pltpu.VMEM((6, 6, 8, 16, 128), jnp.bfloat16),
            pltpu.VMEM((6, 6, 6, 8, 16, 128), jnp.bfloat16),
            pltpu.VMEM((3, 8, 16, 128), F32),
            pltpu.VMEM((8, 16, 128), F32),
            pltpu.VMEM((8, 16, 128), F32),
            pltpu.VMEM((2, 8, 8, 128), F32),
            pltpu.VMEM((2, 2, 8, 8, 128), F32),
            pltpu.VMEM((2, 8, 128), F32),
            pltpu.VMEM((128, 128), F32),
            pltpu.VMEM((16, 128), F32),
            pltpu.SMEM((1,), F32),
            dma((14,)),
            dma((2, 2, 2)),
            dma((2, 2, 2)),
            dma((2, 2, 3)),
            dma((2, 2, 3)),
            dma((2, 2, 3)),
            dma((2, 2, 3)),
            dma((2,)),
            dma((2,)),
            pltpu.SemaphoreType.REGULAR,
            pltpu.SemaphoreType.REGULAR,
        ],
        compiler_params=pltpu.CompilerParams(
            collective_id=0, has_side_effects=True, vmem_limit_bytes=40 * 1024 * 1024
        ),
        name="tangent",
    )(*(
        pltpu.with_memory_space_constraint(operand, pltpu.HBM)
        for operand in (
            guess, right_side, diag_block, neighbour_blocks, dissipation, omega_volume, pseudo_step
        )
    ), phase)
    return field, norms[0, :2]


def solution(mesh):
    placed = (
        P(None, None, "pitch", "span", "axial"),
        P(None, None, "pitch", "span", "axial"),
        P(None, None, "pitch", "span", "axial"),
        P(None, None, None, "pitch", "span", "axial"),
        P(None, "pitch", "span", "axial"),
        P("pitch", "span", "axial"),
        P("pitch", "span", "axial"),
        P(),
    )
    return jax.shard_map(
        body,
        mesh=mesh,
        in_specs=placed,
        out_specs=(P(None, None, "pitch", "span", "axial"), P()),
        check_vma=False,
    )
```
